1024 devices in a mesh: energy: 64 (over y, z_lo, core), kz: 16 (over x, z_hi).
Axes of the slice: x: 4, y: 4, z: 32 (z_hi: 4, z_lo: 8; z = z_hi * 8 + z_lo), core: 2. Of those that a mesh axis runs over, the one named last changes fastest.
Arguments:
- g_less: bfloat16 [16, 192, 1, 2, 128, 128], P('kz', 'energy'), may hold values from -6 to 6
- g_ret: bfloat16 [16, 192, 1, 1, 2, 128, 128], P('kz', 'energy'), may hold values from -0.59765625 to 0.59765625
- neighbors: int32 [1, 32, 4], replicated, may hold values from 0 to 31, as said below
- ph_shift: int32 [2], replicated, may hold values from 1 to 3, as said below
- q_table: int32 [16, 16], replicated, may hold values from 0 to 15
- coupling: float32 [2, 16], replicated, may hold values from 0.2 to 2
- occupation: float32 [2], replicated, may hold values from 0.05 to 3
Outputs:
- g_next: bfloat16 [16, 192, 1, 2, 128, 128], P('kz', 'energy')
The draws below stay inside these ranges and needn't reach their ends.
Inputs may be any that keep to these rules, and one draw needn't show every extreme that they name: `neighbors`: each atom's 4 neighbours are distinct atoms of its slab other than itself. `ph_shift`: the modes' shifts are distinct; one of them is 3.
All inputs are finite; a program needn't handle non-finite values.
Results may differ from the reference program's by a relative error of at most 0.0057.
Values may be sent and summed in bfloat16 or wider, within the bound.
A program may use at most 32 MiB of HBM per device.

```python
import math
import jax
import jax.numpy as jnp
from jax import lax

B = 128
ORB = 4
NB = 4
NMODE = 2
NS = 1
ATOMS = 32
NP = 5
F = 5120
KZ = 16
EN = 192
SMAX = 3


def draw_neighbors(key, part):
    keys = jax.random.split(jax.random.fold_in(key, 11), NS * ATOMS)

    def one_row(row_key):
        return jax.random.permutation(row_key, ATOMS - 1)[:NB]
    offsets = jax.vmap(one_row)(keys).reshape(NS, ATOMS, NB).astype(jnp.int32)
    return ((jnp.arange(ATOMS, dtype=jnp.int32)[None, :, None] + 1 + offsets) % ATOMS).astype(jnp.int32)


def draw_ph_shift(key, part):
    first, second = jax.random.split(jax.random.fold_in(key, 23))
    other = jax.random.randint(first, (), 1, SMAX)
    where_top = jax.random.randint(second, (), 0, NMODE)
    return jnp.where(jnp.arange(NMODE) == where_top, SMAX, other).astype(jnp.int32)


def plant(drawn, stream_key, smallest, high):
    longest = drawn.shape.index(max(drawn.shape))
    spots = []
    for shift in (0, 1):
        where = [jax.random.randint(jax.random.fold_in(stream_key, axis), (), 0, length) for axis, length in enumerate(drawn.shape)]
        where[longest] = (where[longest] + shift) % drawn.shape[longest]
        spots.append(tuple(where))
    return drawn.at[spots[0]].set(smallest).at[spots[1]].set(high)


def block_scale(key, shape, shards, least, top_value):
    def one(axis_at, parts):
        steps = jax.random.uniform(jax.random.fold_in(jax.random.fold_in(key, 6), axis_at), (parts,), jnp.float32, least / len(shards), top_value / len(shards))
        return jnp.repeat(jnp.exp(steps), shape[axis_at] // parts).reshape((-1,) + (1,) * (len(shape) - axis_at - 1))

    gain = one(*shards[0])
    for cut in shards[1:]:
        gain = gain * one(*cut)
    return gain


def centred(key, extent, scale, limit, shards=(), held_as=jnp.bfloat16):
    factor_of = block_scale(key, extent, shards, -0.22, 0.18) if shards else 1.0
    values = jax.random.normal(key, extent, jnp.float32) * scale * factor_of
    return jnp.minimum(jnp.maximum(values, -limit), limit).astype(held_as)


def setup_inputs(seed: int = 0) -> dict:
    key_of = jax.random.split(jax.random.key(seed), 8)
    return {
        "g_less": centred(key_of[0], (KZ, EN, NS, 2, B, B), 1.0, 6.0, ((0, 16), (1, 64))),
        "g_ret": centred(key_of[1], (KZ, EN, NS, NS, 2, B, B), 0.1, 0.59765625, ((0, 16), (1, 64))),
        "neighbors": draw_neighbors(jax.random.fold_in(key_of[7], 71), 0),
        "ph_shift": draw_ph_shift(jax.random.fold_in(key_of[7], 71), 0),
        "q_table": plant(jax.random.randint(key_of[4], (KZ, KZ), 0, KZ), jax.random.fold_in(key_of[4], 1), 0, KZ - 1).astype(jnp.int32),
        "coupling": jnp.clip(jnp.exp(jax.random.uniform(key_of[5], (NMODE, KZ), jnp.float32, math.log(0.2), math.log(2.0))), 0.2, 2.0),
        "occupation": jnp.clip(jnp.exp(jax.random.uniform(key_of[6], (NMODE,), jnp.float32, math.log(0.05), math.log(3.0))), 0.05, 3.0),
    }


def selection(neighbors, atoms, kind):
    own = jnp.broadcast_to(jnp.arange(atoms, dtype=jnp.int32)[None, :, None], (neighbors.shape[0], atoms, 1))
    pairs = jnp.concatenate([own, neighbors.astype(jnp.int32)], axis=2)
    return (pairs[..., None] == jnp.arange(atoms, dtype=jnp.int32)).astype(kind)


def reference(g_less, g_ret, neighbors, ph_shift, q_table, coupling, occupation):
    select = selection(neighbors, ATOMS, jnp.float32)

    def pick(green):
        blocks = green.astype(jnp.float32).reshape(EN, NS, 2, ATOMS, ORB, ATOMS, ORB)
        return jnp.einsum('esnaobp,sajb->esnaojp', blocks, select).reshape(EN, NS, F)

    picked = lax.map(pick, g_less)
    padded = jnp.pad(picked, ((0, 0), (SMAX, SMAX), (0, 0), (0, 0)))
    table = coupling[:, q_table] / KZ
    sigma = jnp.zeros((KZ, EN, NS, F), jnp.float32)
    for mode in range(NMODE):
        lower = lax.dynamic_slice_in_dim(padded, (SMAX - ph_shift[mode]).astype(jnp.int32), EN, 1)
        upper = lax.dynamic_slice_in_dim(padded, (SMAX + ph_shift[mode]).astype(jnp.int32), EN, 1)
        sigma = sigma + jnp.einsum('kq,qesf->kesf', table[mode] * occupation[mode], lower, precision=lax.Precision.HIGHEST)
        sigma = sigma + jnp.einsum('kq,qesf->kesf', table[mode] * (occupation[mode] + 1.0), upper, precision=lax.Precision.HIGHEST)
    sigma = sigma.astype(jnp.bfloat16)

    def keldysh(pair):
        retarded, self_energy = pair
        dense = jnp.einsum('esnaojp,sajb->esnaobp', self_energy.astype(jnp.float32).reshape(EN, NS, 2, ATOMS, ORB, NP, ORB), select)
        dense = dense.reshape(EN, NS, 2, B, B)
        green = retarded.astype(jnp.float32)
        green_re = green[:, :, :, 0]
        green_im = green[:, :, :, 1]
        sig_re = dense[:, :, 0]
        sig_im = dense[:, :, 1]
        prod_re = jnp.einsum('estij,etjk->estik', green_re, sig_re) - jnp.einsum('estij,etjk->estik', green_im, sig_im)
        prod_im = jnp.einsum('estij,etjk->estik', green_re, sig_im) + jnp.einsum('estij,etjk->estik', green_im, sig_re)
        prod_re = lax.optimization_barrier(prod_re.astype(jnp.bfloat16)).astype(jnp.float32)
        prod_im = lax.optimization_barrier(prod_im.astype(jnp.bfloat16)).astype(jnp.float32)
        real_part = jnp.einsum('estik,estlk->esil', prod_re, green_re) + jnp.einsum('estik,estlk->esil', prod_im, green_im)
        imag_part = jnp.einsum('estik,estlk->esil', prod_im, green_re) - jnp.einsum('estik,estlk->esil', prod_re, green_im)
        return jnp.stack([real_part, imag_part], axis=2).astype(jnp.bfloat16)

    return lax.map(keldysh, (g_ret, sigma))
```

```python
import jax
import jax.numpy as jnp
from jax import lax
from jax.sharding import PartitionSpec as P

ORB = 4
NMODE = 2
ZHI = 4


def padded(cells, axis, dim, width):
    count = lax.axis_size(axis)
    ends = count - 1
    head = lax.slice_in_dim(cells, 0, width, axis=dim)
    tail = lax.slice_in_dim(cells, cells.shape[dim] - width, cells.shape[dim], axis=dim)
    return jnp.concatenate(
        [
            lax.ppermute(tail, axis, [(i, (i + 1) % count) for i in range(ends)]),
            cells,
            lax.ppermute(head, axis, [((i + 1) % count, i) for i in range(ends)]),
        ],
        axis=dim,
    )


def masks(neighbors, width):
    atoms = width // ORB
    own = jnp.arange(atoms, dtype=jnp.int32)[:, None]
    pairs = jnp.concatenate([own, neighbors[0]], axis=1)
    row_pairs = jnp.repeat(pairs, ORB, axis=0)
    col_atom = jnp.arange(width, dtype=jnp.int32) // ORB
    return (row_pairs.T[:, :, None] == col_atom[None, None, :]).astype(jnp.bfloat16)


def spread(width):
    return (jnp.arange(width)[:, None] % ORB == jnp.arange(ORB)[None, :]).astype(jnp.bfloat16)


def lookup(table, rows, cols):
    size = table.shape[0]
    r = (rows[:, None] == jnp.arange(size)[None, :]).astype(jnp.float32)
    c = (cols[:, None] == jnp.arange(size)[None, :]).astype(jnp.float32)
    t = table.astype(jnp.float32)
    return jnp.dot(jnp.dot(r, t, precision=lax.Precision.HIGHEST), c.T, precision=lax.Precision.HIGHEST)


def per_device(g_less, g_ret, neighbors, ph_shift, q_table, coupling, occupation):
    edev = g_less.shape[1]
    width = g_less.shape[4]
    members = neighbors.shape[2] + 1
    momenta = lax.axis_size("kz")
    xs = momenta // ZHI
    mask = masks(neighbors, width)
    e4 = spread(width)

    green = g_less[0, :, 0]
    held = green[:, :, None] * mask[None, None]
    picked = jnp.einsum("enjrc,cp->enjpr", held, e4, preferred_element_type=jnp.float32)
    picked = picked.astype(jnp.bfloat16).reshape(edev, 2 * members * ORB, width)

    window = padded(picked, "energy", 0, edev)
    blocks = [window]
    for d in range(1, xs):
        blocks.append(lax.ppermute(window, "kz", [(i, (i + d * ZHI) % momenta) for i in range(momenta)]))
    gathered = jnp.stack(blocks, 0)

    me = lax.axis_index("kz")
    x = me // ZHI
    h = me % ZHI
    dest = x * ZHI + (h + jnp.arange(ZHI)) % ZHI
    src = ((x - jnp.arange(xs)) % xs) * ZHI + h
    qsub = lookup(q_table, dest, src).astype(jnp.int32)
    onehot = (qsub[:, :, None] == jnp.arange(coupling.shape[1])[None, None, :]).astype(jnp.float32)
    weights = jnp.einsum("zdq,mq->mzd", onehot, coupling, precision=lax.Precision.HIGHEST) / momenta

    partial = jnp.zeros((ZHI, edev) + picked.shape[1:], jnp.float32)
    for mode in range(NMODE):
        lower = lax.dynamic_slice_in_dim(gathered, edev - ph_shift[mode], edev, 1).astype(jnp.float32)
        upper = lax.dynamic_slice_in_dim(gathered, edev + ph_shift[mode], edev, 1).astype(jnp.float32)
        partial = partial + jnp.einsum(
            "zd,derb->zerb", weights[mode] * occupation[mode], lower, precision=lax.Precision.HIGHEST
        )
        partial = partial + jnp.einsum(
            "zd,derb->zerb", weights[mode] * (occupation[mode] + 1.0), upper, precision=lax.Precision.HIGHEST
        )

    total = partial[0]
    for d in range(1, ZHI):
        pairs = [(i, (i // ZHI) * ZHI + (i % ZHI + d) % ZHI) for i in range(momenta)]
        total = total + lax.ppermute(partial[d], "kz", pairs)
    sigma = total.astype(jnp.bfloat16).reshape(edev, 2, members, ORB, width)

    tiled = jnp.einsum("enjpr,cp->enjrc", sigma, e4, preferred_element_type=jnp.float32)
    dense = jnp.sum(tiled * mask[None, None].astype(jnp.float32), axis=2).astype(jnp.bfloat16)

    greenr = g_ret[0, :, 0, 0]
    green_re = greenr[:, 0]
    green_im = greenr[:, 1]
    sig_re = dense[:, 0]
    sig_im = dense[:, 1]
    prod_re = jnp.einsum("eij,ejk->eik", green_re, sig_re, preferred_element_type=jnp.float32)
    prod_re = prod_re - jnp.einsum("eij,ejk->eik", green_im, sig_im, preferred_element_type=jnp.float32)
    prod_im = jnp.einsum("eij,ejk->eik", green_re, sig_im, preferred_element_type=jnp.float32)
    prod_im = prod_im + jnp.einsum("eij,ejk->eik", green_im, sig_re, preferred_element_type=jnp.float32)
    prod_re = prod_re.astype(jnp.bfloat16)
    prod_im = prod_im.astype(jnp.bfloat16)
    real_part = jnp.einsum("eik,elk->eil", prod_re, green_re, preferred_element_type=jnp.float32)
    real_part = real_part + jnp.einsum("eik,elk->eil", prod_im, green_im, preferred_element_type=jnp.float32)
    imag_part = jnp.einsum("eik,elk->eil", prod_im, green_re, preferred_element_type=jnp.float32)
    imag_part = imag_part - jnp.einsum("eik,elk->eil", prod_re, green_im, preferred_element_type=jnp.float32)
    result = jnp.stack([real_part, imag_part], axis=1).astype(jnp.bfloat16)
    return result[None, :, None]


def solution(mesh):
    placed = (
        P("kz", "energy", None, None, None, None),
        P("kz", "energy", None, None, None, None, None),
        P(),
        P(),
        P(),
        P(),
        P(),
    )
    return jax.shard_map(
        per_device,
        mesh=mesh,
        in_specs=placed,
        out_specs=P("kz", "energy", None, None, None, None),
        check_vma=False,
    )
```

```python
import jax
import jax.numpy as jnp
from jax import lax
from jax.experimental import pallas as pl
from jax.experimental.pallas import tpu as pltpu
from jax.sharding import PartitionSpec as P

ORB = 4
NMODE = 2
ZHI = 4


def padded(cells, axis, dim, width):
    count = lax.axis_size(axis)
    ends = count - 1
    head = lax.slice_in_dim(cells, 0, width, axis=dim)
    tail = lax.slice_in_dim(cells, cells.shape[dim] - width, cells.shape[dim], axis=dim)
    return jnp.concatenate(
        [
            lax.ppermute(tail, axis, [(i, (i + 1) % count) for i in range(ends)]),
            cells,
            lax.ppermute(head, axis, [((i + 1) % count, i) for i in range(ends)]),
        ],
        axis=dim,
    )


def masks(neighbors, width):
    atoms = width // ORB
    own = jnp.arange(atoms, dtype=jnp.int32)[:, None]
    pairs = jnp.concatenate([own, neighbors[0]], axis=1)
    row_pairs = jnp.repeat(pairs, ORB, axis=0)
    col_atom = jnp.arange(width, dtype=jnp.int32) // ORB
    return (row_pairs.T[:, :, None] == col_atom[None, None, :]).astype(jnp.bfloat16)


def spread(width):
    return (jnp.arange(width)[:, None] % ORB == jnp.arange(ORB)[None, :]).astype(jnp.bfloat16)


def lookup(table, rows, cols):
    size = table.shape[0]
    r = (rows[:, None] == jnp.arange(size)[None, :]).astype(jnp.float32)
    c = (cols[:, None] == jnp.arange(size)[None, :]).astype(jnp.float32)
    t = table.astype(jnp.float32)
    return jnp.dot(jnp.dot(r, t, precision=lax.Precision.HIGHEST), c.T, precision=lax.Precision.HIGHEST)


def exchange_kernel(part_ref, out_ref, near_r, near_l, relay_r, relay_l, far_r, far_l, send, recv):
    me = lax.axis_index("kz")
    x = me // ZHI
    h = me % ZHI
    right = x * ZHI + (h + 1) % ZHI
    left = x * ZHI + (h + ZHI - 1) % ZHI
    mesh = pl.DeviceIdType.MESH
    barrier = pltpu.get_barrier_semaphore()
    for nb in (left, right):
        pl.semaphore_signal(barrier, 1, device_id={"kz": nb}, device_id_type=mesh)
    pl.semaphore_wait(barrier, 2)
    half = part_ref.shape[1] // 2

    def remote(src, dst, slot, to):
        return pltpu.make_async_remote_copy(
            src_ref=src, dst_ref=dst, send_sem=send.at[slot], recv_sem=recv.at[slot],
            device_id={"kz": to}, device_id_type=mesh,
        )

    to_right = remote(part_ref.at[1], near_r, 0, right)
    to_left = remote(part_ref.at[ZHI - 1], near_l, 1, left)
    relay_right = remote(part_ref.at[2, pl.ds(0, half)], relay_r, 2, right)
    relay_left = remote(part_ref.at[2, pl.ds(half, half)], relay_l, 3, left)
    for c in (to_right, to_left, relay_right, relay_left):
        c.start()
    relay_right.wait_recv()
    fwd_right = remote(relay_r, far_r, 4, right)
    fwd_right.start()
    relay_left.wait_recv()
    fwd_left = remote(relay_l, far_l, 5, left)
    fwd_left.start()
    to_right.wait()
    to_left.wait()
    relay_right.wait_send()
    relay_left.wait_send()
    fwd_right.wait()
    fwd_left.wait()
    total = part_ref[0] + near_r[...] + near_l[...]
    out_ref[pl.ds(0, half)] = (total[:half] + far_r[...]).astype(out_ref.dtype)
    out_ref[pl.ds(half, half)] = (total[half:] + far_l[...]).astype(out_ref.dtype)


def exchange(partial):
    _, rows, lanes = partial.shape
    half = rows // 2
    vmem = pltpu.VMEM
    return pl.pallas_call(
        exchange_kernel,
        out_shape=jax.ShapeDtypeStruct((rows, lanes), jnp.bfloat16),
        in_specs=[pl.BlockSpec(memory_space=vmem)],
        out_specs=pl.BlockSpec(memory_space=vmem),
        scratch_shapes=[
            vmem((rows, lanes), jnp.float32),
            vmem((rows, lanes), jnp.float32),
            vmem((half, lanes), jnp.float32),
            vmem((half, lanes), jnp.float32),
            vmem((half, lanes), jnp.float32),
            vmem((half, lanes), jnp.float32),
            pltpu.SemaphoreType.DMA((6,)),
            pltpu.SemaphoreType.DMA((6,)),
        ],
        compiler_params=pltpu.CompilerParams(collective_id=0, has_side_effects=True),
    )(partial)


def per_device(g_less, g_ret, neighbors, ph_shift, q_table, coupling, occupation):
    edev = g_less.shape[1]
    width = g_less.shape[4]
    members = neighbors.shape[2] + 1
    momenta = lax.axis_size("kz")
    xs = momenta // ZHI
    mask = masks(neighbors, width)
    e4 = spread(width)

    green = g_less[0, :, 0]
    held = green[:, :, None] * mask[None, None]
    picked = jnp.einsum("enjrc,cp->enjpr", held, e4, preferred_element_type=jnp.float32)
    picked = picked.astype(jnp.bfloat16).reshape(edev, 2 * members * ORB, width)

    window = padded(picked, "energy", 0, edev)
    blocks = [window]
    for d in range(1, xs):
        blocks.append(lax.ppermute(window, "kz", [(i, (i + d * ZHI) % momenta) for i in range(momenta)]))
    gathered = jnp.stack(blocks, 0)

    me = lax.axis_index("kz")
    x = me // ZHI
    h = me % ZHI
    dest = x * ZHI + (h + jnp.arange(ZHI)) % ZHI
    src = ((x - jnp.arange(xs)) % xs) * ZHI + h
    qsub = lookup(q_table, dest, src).astype(jnp.int32)
    onehot = (qsub[:, :, None] == jnp.arange(coupling.shape[1])[None, None, :]).astype(jnp.float32)
    weights = jnp.einsum("zdq,mq->mzd", onehot, coupling, precision=lax.Precision.HIGHEST) / momenta

    partial = jnp.zeros((ZHI, edev) + picked.shape[1:], jnp.float32)
    for mode in range(NMODE):
        lower = lax.dynamic_slice_in_dim(gathered, edev - ph_shift[mode], edev, 1).astype(jnp.float32)
        upper = lax.dynamic_slice_in_dim(gathered, edev + ph_shift[mode], edev, 1).astype(jnp.float32)
        partial = partial + jnp.einsum(
            "zd,derb->zerb", weights[mode] * occupation[mode], lower, precision=lax.Precision.HIGHEST
        )
        partial = partial + jnp.einsum(
            "zd,derb->zerb", weights[mode] * (occupation[mode] + 1.0), upper, precision=lax.Precision.HIGHEST
        )

    sigma = exchange(partial.reshape(ZHI, -1, width))
    sigma = sigma.reshape(edev, 2, members, ORB, width)

    tiled = jnp.einsum("enjpr,cp->enjrc", sigma, e4, preferred_element_type=jnp.float32)
    dense = jnp.sum(tiled * mask[None, None].astype(jnp.float32), axis=2).astype(jnp.bfloat16)

    greenr = g_ret[0, :, 0, 0]
    green_re = greenr[:, 0]
    green_im = greenr[:, 1]
    sig_re = dense[:, 0]
    sig_im = dense[:, 1]
    prod_re = jnp.einsum("eij,ejk->eik", green_re, sig_re, preferred_element_type=jnp.float32)
    prod_re = prod_re - jnp.einsum("eij,ejk->eik", green_im, sig_im, preferred_element_type=jnp.float32)
    prod_im = jnp.einsum("eij,ejk->eik", green_re, sig_im, preferred_element_type=jnp.float32)
    prod_im = prod_im + jnp.einsum("eij,ejk->eik", green_im, sig_re, preferred_element_type=jnp.float32)
    prod_re = prod_re.astype(jnp.bfloat16)
    prod_im = prod_im.astype(jnp.bfloat16)
    real_part = jnp.einsum("eik,elk->eil", prod_re, green_re, preferred_element_type=jnp.float32)
    real_part = real_part + jnp.einsum("eik,elk->eil", prod_im, green_im, preferred_element_type=jnp.float32)
    imag_part = jnp.einsum("eik,elk->eil", prod_im, green_re, preferred_element_type=jnp.float32)
    imag_part = imag_part - jnp.einsum("eik,elk->eil", prod_re, green_im, preferred_element_type=jnp.float32)
    result = jnp.stack([real_part, imag_part], axis=1).astype(jnp.bfloat16)
    return result[None, :, None]


def solution(mesh):
    placed = (
        P("kz", "energy", None, None, None, None),
        P("kz", "energy", None, None, None, None, None),
        P(),
        P(),
        P(),
        P(),
        P(),
    )
    return jax.shard_map(
        per_device,
        mesh=mesh,
        in_specs=placed,
        out_specs=P("kz", "energy", None, None, None, None),
        check_vma=False,
    )
```

```python
import jax
import jax.numpy as jnp
from jax import lax
from jax.experimental import pallas as pl
from jax.experimental.pallas import tpu as pltpu
from jax.sharding import PartitionSpec as P

ORB = 4
NMODE = 2
ZHI = 4


def padded(cells, axis, dim, width):
    count = lax.axis_size(axis)
    ends = count - 1
    head = lax.slice_in_dim(cells, 0, width, axis=dim)
    tail = lax.slice_in_dim(cells, cells.shape[dim] - width, cells.shape[dim], axis=dim)
    return jnp.concatenate(
        [
            lax.ppermute(tail, axis, [(i, (i + 1) % count) for i in range(ends)]),
            cells,
            lax.ppermute(head, axis, [((i + 1) % count, i) for i in range(ends)]),
        ],
        axis=dim,
    )


def masks(neighbors, width):
    atoms = width // ORB
    own = jnp.arange(atoms, dtype=jnp.int32)[:, None]
    pairs = jnp.concatenate([own, neighbors[0]], axis=1)
    row_pairs = jnp.repeat(pairs, ORB, axis=0)
    col_atom = jnp.arange(width, dtype=jnp.int32) // ORB
    return (row_pairs.T[:, :, None] == col_atom[None, None, :]).astype(jnp.bfloat16)


def spread(width):
    return (jnp.arange(width)[:, None] % ORB == jnp.arange(ORB)[None, :]).astype(jnp.bfloat16)


def lookup(table, rows, cols):
    size = table.shape[0]
    r = (rows[:, None] == jnp.arange(size)[None, :]).astype(jnp.float32)
    c = (cols[:, None] == jnp.arange(size)[None, :]).astype(jnp.float32)
    t = table.astype(jnp.float32)
    return jnp.dot(jnp.dot(r, t, precision=lax.Precision.HIGHEST), c.T, precision=lax.Precision.HIGHEST)


def exchange_kernel(part_ref, out_ref, relay_r, relay_l, near_r, near_l, far_r, far_l, sum_r, sum_l, send, recv):
    me = lax.axis_index("kz")
    x = me // ZHI
    h = me % ZHI
    right = x * ZHI + (h + 1) % ZHI
    left = x * ZHI + (h + ZHI - 1) % ZHI
    mesh = pl.DeviceIdType.MESH
    barrier = pltpu.get_barrier_semaphore()
    for nb in (left, right):
        pl.semaphore_signal(barrier, 1, device_id={"kz": nb}, device_id_type=mesh)
    pl.semaphore_wait(barrier, 2)
    half = part_ref.shape[1] // 2
    lo = pl.ds(0, half)
    hi = pl.ds(half, half)

    def remote(src, dst, slot, to):
        return pltpu.make_async_remote_copy(
            src_ref=src, dst_ref=dst, send_sem=send.at[slot], recv_sem=recv.at[slot],
            device_id={"kz": to}, device_id_type=mesh,
        )

    far_right = remote(part_ref.at[2, lo], relay_r, 0, right)
    far_left = remote(part_ref.at[2, hi], relay_l, 1, left)
    plain_right = remote(part_ref.at[1, hi], near_r, 2, right)
    plain_left = remote(part_ref.at[ZHI - 1, lo], near_l, 3, left)
    for c in (far_right, far_left, plain_right, plain_left):
        c.start()
    far_right.wait_recv()
    sum_r[...] = relay_r[...] + part_ref[1, lo]
    merged_right = remote(sum_r, far_r, 4, right)
    merged_right.start()
    far_left.wait_recv()
    sum_l[...] = relay_l[...] + part_ref[ZHI - 1, hi]
    merged_left = remote(sum_l, far_l, 5, left)
    merged_left.start()
    plain_right.wait()
    plain_left.wait()
    far_right.wait_send()
    far_left.wait_send()
    merged_right.wait()
    merged_left.wait()
    out_ref[lo] = (part_ref[0, lo] + near_l[...] + far_r[...]).astype(out_ref.dtype)
    out_ref[hi] = (part_ref[0, hi] + near_r[...] + far_l[...]).astype(out_ref.dtype)


def exchange(partial):
    _, rows, lanes = partial.shape
    half = rows // 2
    vmem = pltpu.VMEM
    return pl.pallas_call(
        exchange_kernel,
        out_shape=jax.ShapeDtypeStruct((rows, lanes), jnp.bfloat16),
        in_specs=[pl.BlockSpec(memory_space=vmem)],
        out_specs=pl.BlockSpec(memory_space=vmem),
        scratch_shapes=[vmem((half, lanes), jnp.float32) for _ in range(8)]
        + [pltpu.SemaphoreType.DMA((6,)), pltpu.SemaphoreType.DMA((6,))],
        compiler_params=pltpu.CompilerParams(collective_id=0, has_side_effects=True),
    )(partial)


def per_device(g_less, g_ret, neighbors, ph_shift, q_table, coupling, occupation):
    edev = g_less.shape[1]
    width = g_less.shape[4]
    members = neighbors.shape[2] + 1
    momenta = lax.axis_size("kz")
    xs = momenta // ZHI
    mask = masks(neighbors, width)
    e4 = spread(width)

    green = g_less[0, :, 0]
    held = green[:, :, None] * mask[None, None]
    picked = jnp.einsum("enjrc,cp->enjpr", held, e4, preferred_element_type=jnp.float32)
    picked = picked.astype(jnp.bfloat16).reshape(edev, 2 * members * ORB, width)

    window = padded(picked, "energy", 0, edev)
    blocks = [window]
    for d in range(1, xs):
        blocks.append(lax.ppermute(window, "kz", [(i, (i + d * ZHI) % momenta) for i in range(momenta)]))
    gathered = jnp.stack(blocks, 0)

    me = lax.axis_index("kz")
    x = me // ZHI
    h = me % ZHI
    dest = x * ZHI + (h + jnp.arange(ZHI)) % ZHI
    src = ((x - jnp.arange(xs)) % xs) * ZHI + h
    qsub = lookup(q_table, dest, src).astype(jnp.int32)
    onehot = (qsub[:, :, None] == jnp.arange(coupling.shape[1])[None, None, :]).astype(jnp.float32)
    weights = jnp.einsum("zdq,mq->mzd", onehot, coupling, precision=lax.Precision.HIGHEST) / momenta

    partial = jnp.zeros((ZHI, edev) + picked.shape[1:], jnp.float32)
    for mode in range(NMODE):
        lower = lax.dynamic_slice_in_dim(gathered, edev - ph_shift[mode], edev, 1).astype(jnp.float32)
        upper = lax.dynamic_slice_in_dim(gathered, edev + ph_shift[mode], edev, 1).astype(jnp.float32)
        partial = partial + jnp.einsum(
            "zd,derb->zerb", weights[mode] * occupation[mode], lower, precision=lax.Precision.HIGHEST
        )
        partial = partial + jnp.einsum(
            "zd,derb->zerb", weights[mode] * (occupation[mode] + 1.0), upper, precision=lax.Precision.HIGHEST
        )

    sigma = exchange(partial.reshape(ZHI, -1, width))
    sigma = sigma.reshape(edev, 2, members, ORB, width)

    tiled = jnp.einsum("enjpr,cp->enjrc", sigma, e4, preferred_element_type=jnp.float32)
    dense = jnp.sum(tiled * mask[None, None].astype(jnp.float32), axis=2).astype(jnp.bfloat16)

    greenr = g_ret[0, :, 0, 0]
    green_re = greenr[:, 0]
    green_im = greenr[:, 1]
    sig_re = dense[:, 0]
    sig_im = dense[:, 1]
    prod_re = jnp.einsum("eij,ejk->eik", green_re, sig_re, preferred_element_type=jnp.float32)
    prod_re = prod_re - jnp.einsum("eij,ejk->eik", green_im, sig_im, preferred_element_type=jnp.float32)
    prod_im = jnp.einsum("eij,ejk->eik", green_re, sig_im, preferred_element_type=jnp.float32)
    prod_im = prod_im + jnp.einsum("eij,ejk->eik", green_im, sig_re, preferred_element_type=jnp.float32)
    prod_re = prod_re.astype(jnp.bfloat16)
    prod_im = prod_im.astype(jnp.bfloat16)
    real_part = jnp.einsum("eik,elk->eil", prod_re, green_re, preferred_element_type=jnp.float32)
    real_part = real_part + jnp.einsum("eik,elk->eil", prod_im, green_im, preferred_element_type=jnp.float32)
    imag_part = jnp.einsum("eik,elk->eil", prod_im, green_re, preferred_element_type=jnp.float32)
    imag_part = imag_part - jnp.einsum("eik,elk->eil", prod_re, green_im, preferred_element_type=jnp.float32)
    result = jnp.stack([real_part, imag_part], axis=1).astype(jnp.bfloat16)
    return result[None, :, None]


def solution(mesh):
    placed = (
        P("kz", "energy", None, None, None, None),
        P("kz", "energy", None, None, None, None, None),
        P(),
        P(),
        P(),
        P(),
        P(),
    )
    return jax.shard_map(
        per_device,
        mesh=mesh,
        in_specs=placed,
        out_specs=P("kz", "energy", None, None, None, None),
        check_vma=False,
    )
```

```python
import jax
import jax.numpy as jnp
from jax import lax
from jax.experimental import pallas as pl
from jax.experimental.pallas import tpu as pltpu
from jax.sharding import PartitionSpec as P

ORB = 4
NMODE = 2
ZHI = 4


def masks(neighbors, width):
    atoms = width // ORB
    own = jnp.arange(atoms, dtype=jnp.int32)[:, None]
    pairs = jnp.concatenate([own, neighbors[0]], axis=1)
    row_pairs = jnp.repeat(pairs, ORB, axis=0)
    col_atom = jnp.arange(width, dtype=jnp.int32) // ORB
    return (row_pairs.T[:, :, None] == col_atom[None, None, :]).astype(jnp.bfloat16)


def spread(width):
    return (jnp.arange(width)[:, None] % ORB == jnp.arange(ORB)[None, :]).astype(jnp.bfloat16)


def lookup(table, rows, cols):
    size = table.shape[0]
    r = (rows[:, None] == jnp.arange(size)[None, :]).astype(jnp.float32)
    c = (cols[:, None] == jnp.arange(size)[None, :]).astype(jnp.float32)
    t = table.astype(jnp.float32)
    return jnp.dot(jnp.dot(r, t, precision=lax.Precision.HIGHEST), c.T, precision=lax.Precision.HIGHEST)


def exchange_kernel(part_ref, out_ref, relay_r, relay_l, near_r, near_l, far_r, far_l, sum_r, sum_l, send, recv):
    me = lax.axis_index("kz")
    x = me // ZHI
    h = me % ZHI
    right = x * ZHI + (h + 1) % ZHI
    left = x * ZHI + (h + ZHI - 1) % ZHI
    mesh = pl.DeviceIdType.MESH
    barrier = pltpu.get_barrier_semaphore()
    for nb in (left, right):
        pl.semaphore_signal(barrier, 1, device_id={"kz": nb}, device_id_type=mesh)
    pl.semaphore_wait(barrier, 2)
    half = part_ref.shape[1] // 2
    lo = pl.ds(0, half)
    hi = pl.ds(half, half)

    def remote(src, dst, slot, to):
        return pltpu.make_async_remote_copy(
            src_ref=src, dst_ref=dst, send_sem=send.at[slot], recv_sem=recv.at[slot],
            device_id={"kz": to}, device_id_type=mesh,
        )

    far_right = remote(part_ref.at[2, lo], relay_r, 0, right)
    far_left = remote(part_ref.at[2, hi], relay_l, 1, left)
    plain_right = remote(part_ref.at[1, hi], near_r, 2, right)
    plain_left = remote(part_ref.at[ZHI - 1, lo], near_l, 3, left)
    for c in (far_right, far_left, plain_right, plain_left):
        c.start()
    far_right.wait_recv()
    sum_r[...] = relay_r[...] + part_ref[1, lo]
    merged_right = remote(sum_r, far_r, 4, right)
    merged_right.start()
    far_left.wait_recv()
    sum_l[...] = relay_l[...] + part_ref[ZHI - 1, hi]
    merged_left = remote(sum_l, far_l, 5, left)
    merged_left.start()
    plain_right.wait()
    plain_left.wait()
    far_right.wait_send()
    far_left.wait_send()
    merged_right.wait()
    merged_left.wait()
    out_ref[lo] = (part_ref[0, lo] + near_l[...] + far_r[...]).astype(out_ref.dtype)
    out_ref[hi] = (part_ref[0, hi] + near_r[...] + far_l[...]).astype(out_ref.dtype)


def exchange(partial):
    _, rows, lanes = partial.shape
    half = rows // 2
    vmem = pltpu.VMEM
    return pl.pallas_call(
        exchange_kernel,
        out_shape=jax.ShapeDtypeStruct((rows, lanes), jnp.bfloat16),
        in_specs=[pl.BlockSpec(memory_space=vmem)],
        out_specs=pl.BlockSpec(memory_space=vmem),
        scratch_shapes=[vmem((half, lanes), jnp.float32) for _ in range(8)]
        + [pltpu.SemaphoreType.DMA((6,)), pltpu.SemaphoreType.DMA((6,))],
        compiler_params=pltpu.CompilerParams(collective_id=0, has_side_effects=True),
    )(partial)


def gather_kernel(own_ref, out_ref, land, send, recv):
    kz = lax.axis_index("kz")
    eb = lax.axis_index("energy")
    ne = lax.axis_size("energy")
    xs = lax.axis_size("kz") // ZHI
    x = kz // ZHI
    h = kz % ZHI
    mesh = pl.DeviceIdType.MESH
    peers = [(d, t) for d in range(xs) for t in (-1, 0, 1) if (d, t) != (0, 0)]

    def where(d, t):
        return {"kz": ((x + d) % xs) * ZHI + h, "energy": (eb + t + ne) % ne}

    barrier = pltpu.get_barrier_semaphore()
    for d, t in peers:
        pl.semaphore_signal(barrier, 1, device_id=where(d, t), device_id_type=mesh)
    pl.semaphore_wait(barrier, len(peers))
    copies = []
    for i, (d, t) in enumerate(peers):
        c = pltpu.make_async_remote_copy(
            src_ref=own_ref, dst_ref=land.at[d, 1 - t], send_sem=send.at[i], recv_sem=recv.at[i],
            device_id=where(d, t), device_id_type=mesh,
        )
        c.start()
        copies.append(c)
    for c in copies:
        c.wait()
    zero = jnp.zeros(own_ref.shape, own_ref.dtype)
    for d in range(xs):
        if d == 0:
            out_ref[0, 1] = own_ref[...]
        else:
            out_ref[d, 1] = land[d, 1]
        out_ref[d, 0] = jnp.where(eb > 0, land[d, 0], zero)
        out_ref[d, 2] = jnp.where(eb < ne - 1, land[d, 2], zero)


def gather(own):
    xs = lax.axis_size("kz") // ZHI
    vmem = pltpu.VMEM
    peers = 3 * xs - 1
    return pl.pallas_call(
        gather_kernel,
        out_shape=jax.ShapeDtypeStruct((xs, 3) + own.shape, own.dtype),
        in_specs=[pl.BlockSpec(memory_space=vmem)],
        out_specs=pl.BlockSpec(memory_space=vmem),
        scratch_shapes=[
            vmem((xs, 3) + own.shape, own.dtype),
            pltpu.SemaphoreType.DMA((peers,)),
            pltpu.SemaphoreType.DMA((peers,)),
        ],
        compiler_params=pltpu.CompilerParams(collective_id=1, has_side_effects=True),
    )(own)


def per_device(g_less, g_ret, neighbors, ph_shift, q_table, coupling, occupation):
    edev = g_less.shape[1]
    width = g_less.shape[4]
    members = neighbors.shape[2] + 1
    momenta = lax.axis_size("kz")
    xs = momenta // ZHI
    mask = masks(neighbors, width)
    e4 = spread(width)

    green = g_less[0, :, 0]
    held = green[:, :, None] * mask[None, None]
    picked = jnp.einsum("enjrc,cp->enjpr", held, e4, preferred_element_type=jnp.float32)
    picked = picked.astype(jnp.bfloat16).reshape(edev, 2 * members * ORB, width)

    rows = picked.shape[1]
    gathered = gather(picked.reshape(edev * rows, width))
    gathered = gathered.reshape(xs, 3 * edev, rows, width)

    me = lax.axis_index("kz")
    x = me // ZHI
    h = me % ZHI
    dest = x * ZHI + (h + jnp.arange(ZHI)) % ZHI
    src = ((x - jnp.arange(xs)) % xs) * ZHI + h
    qsub = lookup(q_table, dest, src).astype(jnp.int32)
    onehot = (qsub[:, :, None] == jnp.arange(coupling.shape[1])[None, None, :]).astype(jnp.float32)
    weights = jnp.einsum("zdq,mq->mzd", onehot, coupling, precision=lax.Precision.HIGHEST) / momenta

    partial = jnp.zeros((ZHI, edev) + picked.shape[1:], jnp.float32)
    for mode in range(NMODE):
        lower = lax.dynamic_slice_in_dim(gathered, edev - ph_shift[mode], edev, 1).astype(jnp.float32)
        upper = lax.dynamic_slice_in_dim(gathered, edev + ph_shift[mode], edev, 1).astype(jnp.float32)
        partial = partial + jnp.einsum(
            "zd,derb->zerb", weights[mode] * occupation[mode], lower, precision=lax.Precision.HIGHEST
        )
        partial = partial + jnp.einsum(
            "zd,derb->zerb", weights[mode] * (occupation[mode] + 1.0), upper, precision=lax.Precision.HIGHEST
        )

    sigma = exchange(partial.reshape(ZHI, -1, width))
    sigma = sigma.reshape(edev, 2, members, ORB, width)

    tiled = jnp.einsum("enjpr,cp->enjrc", sigma, e4, preferred_element_type=jnp.float32)
    dense = jnp.sum(tiled * mask[None, None].astype(jnp.float32), axis=2).astype(jnp.bfloat16)

    greenr = g_ret[0, :, 0, 0]
    green_re = greenr[:, 0]
    green_im = greenr[:, 1]
    sig_re = dense[:, 0]
    sig_im = dense[:, 1]
    prod_re = jnp.einsum("eij,ejk->eik", green_re, sig_re, preferred_element_type=jnp.float32)
    prod_re = prod_re - jnp.einsum("eij,ejk->eik", green_im, sig_im, preferred_element_type=jnp.float32)
    prod_im = jnp.einsum("eij,ejk->eik", green_re, sig_im, preferred_element_type=jnp.float32)
    prod_im = prod_im + jnp.einsum("eij,ejk->eik", green_im, sig_re, preferred_element_type=jnp.float32)
    prod_re = prod_re.astype(jnp.bfloat16)
    prod_im = prod_im.astype(jnp.bfloat16)
    real_part = jnp.einsum("eik,elk->eil", prod_re, green_re, preferred_element_type=jnp.float32)
    real_part = real_part + jnp.einsum("eik,elk->eil", prod_im, green_im, preferred_element_type=jnp.float32)
    imag_part = jnp.einsum("eik,elk->eil", prod_im, green_re, preferred_element_type=jnp.float32)
    imag_part = imag_part - jnp.einsum("eik,elk->eil", prod_re, green_im, preferred_element_type=jnp.float32)
    result = jnp.stack([real_part, imag_part], axis=1).astype(jnp.bfloat16)
    return result[None, :, None]


def solution(mesh):
    placed = (
        P("kz", "energy", None, None, None, None),
        P("kz", "energy", None, None, None, None, None),
        P(),
        P(),
        P(),
        P(),
        P(),
    )
    return jax.shard_map(
        per_device,
        mesh=mesh,
        in_specs=placed,
        out_specs=P("kz", "energy", None, None, None, None),
        check_vma=False,
    )
```

```python
import jax
import jax.numpy as jnp
from jax import lax
from jax.experimental import pallas as pl
from jax.experimental.pallas import tpu as pltpu
from jax.sharding import PartitionSpec as P

ORB = 4
NMODE = 2
ZHI = 4


def masks(neighbors, width):
    atoms = width // ORB
    own = jnp.arange(atoms, dtype=jnp.int32)[:, None]
    pairs = jnp.concatenate([own, neighbors[0]], axis=1)
    row_pairs = jnp.repeat(pairs, ORB, axis=0)
    col_atom = jnp.arange(width, dtype=jnp.int32) // ORB
    return (row_pairs.T[:, :, None] == col_atom[None, None, :]).astype(jnp.bfloat16)


def spread(width):
    return (jnp.arange(width)[:, None] % ORB == jnp.arange(ORB)[None, :]).astype(jnp.bfloat16)


def born_kernel(own_ref, q_ref, c_ref, occ_ref, sh_ref, out_ref, land, part, relay_r, relay_l,
                near_r, near_l, far_r, far_l, sum_r, sum_l, gsend, grecv, send, recv):
    kz = lax.axis_index("kz")
    eb = lax.axis_index("energy")
    ne = lax.axis_size("energy")
    momenta = lax.axis_size("kz")
    xs = momenta // ZHI
    x = kz // ZHI
    h = kz % ZHI
    edev = own_ref.shape[0]
    rows = own_ref.shape[1]
    mesh = pl.DeviceIdType.MESH
    peers = [(d, t) for d in range(xs) for t in (-1, 0, 1) if (d, t) != (0, 0)]
    right = x * ZHI + (h + 1) % ZHI
    left = x * ZHI + (h + ZHI - 1) % ZHI

    def where(d, t):
        return {"kz": ((x + d) % xs) * ZHI + h, "energy": (eb + t + ne) % ne}

    barrier = pltpu.get_barrier_semaphore()
    for d, t in peers:
        pl.semaphore_signal(barrier, 1, device_id=where(d, t), device_id_type=mesh)
    for nb in (left, right):
        pl.semaphore_signal(barrier, 1, device_id={"kz": nb}, device_id_type=mesh)
    pl.semaphore_wait(barrier, len(peers) + 2)

    copies = []
    for i, (d, t) in enumerate(peers):
        c = pltpu.make_async_remote_copy(
            src_ref=own_ref, dst_ref=land.at[d, pl.ds((1 - t) * edev, edev)],
            send_sem=gsend.at[i], recv_sem=grecv.at[i], device_id=where(d, t), device_id_type=mesh,
        )
        c.start()
        copies.append(c)
    land[0, pl.ds(edev, edev)] = own_ref[...]
    for c in copies:
        c.wait()
    zero = jnp.zeros((xs, edev) + own_ref.shape[1:], own_ref.dtype)

    @pl.when(eb == 0)
    def _():
        land[:, pl.ds(0, edev)] = zero

    @pl.when(eb == ne - 1)
    def _():
        land[:, pl.ds(2 * edev, edev)] = zero

    shifts = [sh_ref[m] for m in range(NMODE)]
    for z in range(ZHI):
        k = x * ZHI + (h + z) % ZHI
        weights = []
        for d in range(xs):
            q = q_ref[k, ((x - d + xs) % xs) * ZHI + h]
            for m in range(NMODE):
                w = c_ref[m, q] / momenta
                weights.append((d, m, w * occ_ref[m], w * (occ_ref[m] + 1.0)))
        for e in range(edev):
            acc = jnp.zeros(own_ref.shape[1:], jnp.float32)
            for d, m, wl, wu in weights:
                acc = acc + wl * land[d, edev + e - shifts[m]].astype(jnp.float32)
                acc = acc + wu * land[d, edev + e + shifts[m]].astype(jnp.float32)
            part[z, pl.ds(e * rows, rows)] = acc

    half = part.shape[1] // 2
    lo = pl.ds(0, half)
    hi = pl.ds(half, half)

    def remote(src, dst, slot, to):
        return pltpu.make_async_remote_copy(
            src_ref=src, dst_ref=dst, send_sem=send.at[slot], recv_sem=recv.at[slot],
            device_id={"kz": to}, device_id_type=mesh,
        )

    far_right = remote(part.at[2, lo], relay_r, 0, right)
    far_left = remote(part.at[2, hi], relay_l, 1, left)
    plain_right = remote(part.at[1, hi], near_r, 2, right)
    plain_left = remote(part.at[ZHI - 1, lo], near_l, 3, left)
    for c in (far_right, far_left, plain_right, plain_left):
        c.start()
    far_right.wait_recv()
    sum_r[...] = relay_r[...] + part[1, lo]
    merged_right = remote(sum_r, far_r, 4, right)
    merged_right.start()
    far_left.wait_recv()
    sum_l[...] = relay_l[...] + part[ZHI - 1, hi]
    merged_left = remote(sum_l, far_l, 5, left)
    merged_left.start()
    plain_right.wait()
    plain_left.wait()
    far_right.wait_send()
    far_left.wait_send()
    merged_right.wait()
    merged_left.wait()
    out_ref[lo] = (part[0, lo] + near_l[...] + far_r[...]).astype(out_ref.dtype)
    out_ref[hi] = (part[0, hi] + near_r[...] + far_l[...]).astype(out_ref.dtype)


def born(own, q_table, coupling, occupation, ph_shift):
    edev, rows, lanes = own.shape
    xs = lax.axis_size("kz") // ZHI
    half = edev * rows // 2
    vmem = pltpu.VMEM
    smem = pl.BlockSpec(memory_space=pltpu.SMEM)
    return pl.pallas_call(
        born_kernel,
        out_shape=jax.ShapeDtypeStruct((edev * rows, lanes), jnp.bfloat16),
        in_specs=[pl.BlockSpec(memory_space=vmem), smem, smem, smem, smem],
        out_specs=pl.BlockSpec(memory_space=vmem),
        scratch_shapes=[
            vmem((xs, 3 * edev, rows, lanes), own.dtype),
            vmem((ZHI, edev * rows, lanes), jnp.float32),
        ]
        + [vmem((half, lanes), jnp.float32) for _ in range(8)]
        + [
            pltpu.SemaphoreType.DMA((3 * xs - 1,)),
            pltpu.SemaphoreType.DMA((3 * xs - 1,)),
            pltpu.SemaphoreType.DMA((6,)),
            pltpu.SemaphoreType.DMA((6,)),
        ],
        compiler_params=pltpu.CompilerParams(collective_id=0, has_side_effects=True),
    )(own, q_table, coupling, occupation, ph_shift)


def per_device(g_less, g_ret, neighbors, ph_shift, q_table, coupling, occupation):
    edev = g_less.shape[1]
    width = g_less.shape[4]
    members = neighbors.shape[2] + 1
    momenta = lax.axis_size("kz")
    xs = momenta // ZHI
    mask = masks(neighbors, width)
    e4 = spread(width)

    green = g_less[0, :, 0]
    held = green[:, :, None] * mask[None, None]
    picked = jnp.einsum("enjrc,cp->enjpr", held, e4, preferred_element_type=jnp.float32)
    picked = picked.astype(jnp.bfloat16).reshape(edev, 2 * members * ORB, width)
    sigma = born(picked, q_table, coupling, occupation, ph_shift)
    sigma = sigma.reshape(edev, 2, members, ORB, width)

    tiled = jnp.einsum("enjpr,cp->enjrc", sigma, e4, preferred_element_type=jnp.float32)
    dense = jnp.sum(tiled * mask[None, None].astype(jnp.float32), axis=2).astype(jnp.bfloat16)

    greenr = g_ret[0, :, 0, 0]
    green_re = greenr[:, 0]
    green_im = greenr[:, 1]
    sig_re = dense[:, 0]
    sig_im = dense[:, 1]
    prod_re = jnp.einsum("eij,ejk->eik", green_re, sig_re, preferred_element_type=jnp.float32)
    prod_re = prod_re - jnp.einsum("eij,ejk->eik", green_im, sig_im, preferred_element_type=jnp.float32)
    prod_im = jnp.einsum("eij,ejk->eik", green_re, sig_im, preferred_element_type=jnp.float32)
    prod_im = prod_im + jnp.einsum("eij,ejk->eik", green_im, sig_re, preferred_element_type=jnp.float32)
    prod_re = prod_re.astype(jnp.bfloat16)
    prod_im = prod_im.astype(jnp.bfloat16)
    real_part = jnp.einsum("eik,elk->eil", prod_re, green_re, preferred_element_type=jnp.float32)
    real_part = real_part + jnp.einsum("eik,elk->eil", prod_im, green_im, preferred_element_type=jnp.float32)
    imag_part = jnp.einsum("eik,elk->eil", prod_im, green_re, preferred_element_type=jnp.float32)
    imag_part = imag_part - jnp.einsum("eik,elk->eil", prod_re, green_im, preferred_element_type=jnp.float32)
    result = jnp.stack([real_part, imag_part], axis=1).astype(jnp.bfloat16)
    return result[None, :, None]


def solution(mesh):
    placed = (
        P("kz", "energy", None, None, None, None),
        P("kz", "energy", None, None, None, None, None),
        P(),
        P(),
        P(),
        P(),
        P(),
    )
    return jax.shard_map(
        per_device,
        mesh=mesh,
        in_specs=placed,
        out_specs=P("kz", "energy", None, None, None, None),
        check_vma=False,
    )
```

```python
import jax
import jax.numpy as jnp
from jax import lax
from jax.experimental import pallas as pl
from jax.experimental.pallas import tpu as pltpu
from jax.sharding import PartitionSpec as P

ORB = 4
NMODE = 2
ZHI = 4


def masks(neighbors, width):
    atoms = width // ORB
    own = jnp.arange(atoms, dtype=jnp.int32)[:, None]
    pairs = jnp.concatenate([own, neighbors[0]], axis=1)
    row_pairs = jnp.repeat(pairs, ORB, axis=0)
    col_atom = jnp.arange(width, dtype=jnp.int32) // ORB
    return (row_pairs.T[:, :, None] == col_atom[None, None, :]).astype(jnp.bfloat16)


def spread(width):
    return (jnp.arange(width)[:, None] % ORB == jnp.arange(ORB)[None, :]).astype(jnp.bfloat16)


def born_kernel(own_ref, q_ref, c_ref, occ_ref, sh_ref, out_ref, land, landf, part, relay_r, relay_l,
                near_r, near_l, far_r, far_l, sum_r, sum_l, gsend, grecv, send, recv):
    kz = lax.axis_index("kz")
    eb = lax.axis_index("energy")
    ne = lax.axis_size("energy")
    momenta = lax.axis_size("kz")
    xs = momenta // ZHI
    x = kz // ZHI
    h = kz % ZHI
    edev = own_ref.shape[0]
    rows = own_ref.shape[1]
    mesh = pl.DeviceIdType.MESH
    peers = [(d, t) for d in range(xs) for t in (-1, 0, 1) if (d, t) != (0, 0)]
    right = x * ZHI + (h + 1) % ZHI
    left = x * ZHI + (h + ZHI - 1) % ZHI

    def where(d, t):
        return {"kz": ((x + d) % xs) * ZHI + h, "energy": (eb + t + ne) % ne}

    barrier = pltpu.get_barrier_semaphore()
    for d, t in peers:
        pl.semaphore_signal(barrier, 1, device_id=where(d, t), device_id_type=mesh)
    for nb in (left, right):
        pl.semaphore_signal(barrier, 1, device_id={"kz": nb}, device_id_type=mesh)
    pl.semaphore_wait(barrier, len(peers) + 2)

    copies = []
    for i, (d, t) in enumerate(peers):
        c = pltpu.make_async_remote_copy(
            src_ref=own_ref, dst_ref=land.at[d, pl.ds((1 - t) * edev, edev)],
            send_sem=gsend.at[i], recv_sem=grecv.at[i], device_id=where(d, t), device_id_type=mesh,
        )
        c.start()
        copies.append(c)
    for e in range(edev):
        landf[0, edev + e] = own_ref[e].astype(jnp.float32)
    for c in copies:
        c.wait()
    keep = (jnp.where(eb > 0, 1.0, 0.0), 1.0, jnp.where(eb < ne - 1, 1.0, 0.0))
    for d in range(xs):
        for side in range(3):
            if (d, side) == (0, 1):
                continue
            for e in range(edev):
                landf[d, side * edev + e] = land[d, side * edev + e].astype(jnp.float32) * keep[side]

    shifts = [sh_ref[m] for m in range(NMODE)]

    def partial(z):
        k = x * ZHI + (h + z) % ZHI
        weights = []
        for d in range(xs):
            q = q_ref[k, ((x - d + xs) % xs) * ZHI + h]
            for m in range(NMODE):
                w = c_ref[m, q] / momenta
                weights.append((d, m, w * occ_ref[m], w * (occ_ref[m] + 1.0)))
        for e in range(edev):
            acc = jnp.zeros(own_ref.shape[1:], jnp.float32)
            for d, m, wl, wu in weights:
                acc = acc + wl * landf[d, edev + e - shifts[m]]
                acc = acc + wu * landf[d, edev + e + shifts[m]]
            part[z, pl.ds(e * rows, rows)] = acc

    def remote(src, dst, slot, to):
        return pltpu.make_async_remote_copy(
            src_ref=src, dst_ref=dst, send_sem=send.at[slot], recv_sem=recv.at[slot],
            device_id={"kz": to}, device_id_type=mesh,
        )

    total = part.shape[1]
    split = relay_r.shape[0]
    step = split // 2
    chunks_r = [(0, step), (step, split - step)]
    chunks_l = [(0, step), (step, total - split - step)]
    partial(2)
    far_right = [remote(part.at[2, pl.ds(o, n)], relay_r.at[pl.ds(o, n)], i, right)
                 for i, (o, n) in enumerate(chunks_r)]
    far_left = [remote(part.at[2, pl.ds(split + o, n)], relay_l.at[pl.ds(o, n)], 2 + i, left)
                for i, (o, n) in enumerate(chunks_l)]
    for c in far_right + far_left:
        c.start()
    partial(1)
    plain_right = remote(part.at[1, pl.ds(split, total - split)], near_r, 4, right)
    plain_right.start()
    partial(ZHI - 1)
    plain_left = remote(part.at[ZHI - 1, pl.ds(0, split)], near_l, 5, left)
    plain_left.start()
    partial(0)
    merged = []
    for i in range(2):
        o, n = chunks_r[i]
        far_right[i].wait_recv()
        sum_r[pl.ds(o, n)] = relay_r[pl.ds(o, n)] + part[1, pl.ds(o, n)]
        c = remote(sum_r.at[pl.ds(o, n)], far_r.at[pl.ds(o, n)], 6 + i, right)
        c.start()
        merged.append(c)
        o, n = chunks_l[i]
        far_left[i].wait_recv()
        sum_l[pl.ds(o, n)] = relay_l[pl.ds(o, n)] + part[ZHI - 1, pl.ds(split + o, n)]
        c = remote(sum_l.at[pl.ds(o, n)], far_l.at[pl.ds(o, n)], 8 + i, left)
        c.start()
        merged.append(c)
    plain_right.wait()
    plain_left.wait()
    for c in far_right + far_left:
        c.wait_send()
    for c in merged:
        c.wait()
    lo = pl.ds(0, split)
    hi = pl.ds(split, total - split)
    out_ref[lo] = (part[0, lo] + near_l[...] + far_r[...]).astype(out_ref.dtype)
    out_ref[hi] = (part[0, hi] + near_r[...] + far_l[...]).astype(out_ref.dtype)


def born(own, q_table, coupling, occupation, ph_shift):
    edev, rows, lanes = own.shape
    xs = lax.axis_size("kz") // ZHI
    total = edev * rows
    split = (total // 2 + 15) // 16 * 16
    vmem = pltpu.VMEM
    smem = pl.BlockSpec(memory_space=pltpu.SMEM)
    f32 = jnp.float32
    return pl.pallas_call(
        born_kernel,
        out_shape=jax.ShapeDtypeStruct((total, lanes), jnp.bfloat16),
        in_specs=[pl.BlockSpec(memory_space=vmem), smem, smem, smem, smem],
        out_specs=pl.BlockSpec(memory_space=vmem),
        scratch_shapes=[
            vmem((xs, 3 * edev, rows, lanes), own.dtype),
            vmem((xs, 3 * edev, rows, lanes), f32),
            vmem((ZHI, total, lanes), f32),
            vmem((split, lanes), f32),
            vmem((total - split, lanes), f32),
            vmem((total - split, lanes), f32),
            vmem((split, lanes), f32),
            vmem((split, lanes), f32),
            vmem((total - split, lanes), f32),
            vmem((split, lanes), f32),
            vmem((total - split, lanes), f32),
            pltpu.SemaphoreType.DMA((3 * xs - 1,)),
            pltpu.SemaphoreType.DMA((3 * xs - 1,)),
            pltpu.SemaphoreType.DMA((10,)),
            pltpu.SemaphoreType.DMA((10,)),
        ],
        compiler_params=pltpu.CompilerParams(collective_id=0, has_side_effects=True),
    )(own, q_table, coupling, occupation, ph_shift)


def per_device(g_less, g_ret, neighbors, ph_shift, q_table, coupling, occupation):
    edev = g_less.shape[1]
    width = g_less.shape[4]
    members = neighbors.shape[2] + 1
    momenta = lax.axis_size("kz")
    xs = momenta // ZHI
    mask = masks(neighbors, width)
    e4 = spread(width)

    green = g_less[0, :, 0]
    held = green[:, :, None] * mask[None, None]
    picked = jnp.einsum("enjrc,cp->enjpr", held, e4, preferred_element_type=jnp.float32)
    picked = picked.astype(jnp.bfloat16).reshape(edev, 2 * members * ORB, width)
    sigma = born(picked, q_table, coupling, occupation, ph_shift)
    sigma = sigma.reshape(edev, 2, members, ORB, width)

    tiled = jnp.einsum("enjpr,cp->enjrc", sigma, e4, preferred_element_type=jnp.float32)
    dense = jnp.sum(tiled * mask[None, None].astype(jnp.float32), axis=2).astype(jnp.bfloat16)

    greenr = g_ret[0, :, 0, 0]
    green_re = greenr[:, 0]
    green_im = greenr[:, 1]
    sig_re = dense[:, 0]
    sig_im = dense[:, 1]
    prod_re = jnp.einsum("eij,ejk->eik", green_re, sig_re, preferred_element_type=jnp.float32)
    prod_re = prod_re - jnp.einsum("eij,ejk->eik", green_im, sig_im, preferred_element_type=jnp.float32)
    prod_im = jnp.einsum("eij,ejk->eik", green_re, sig_im, preferred_element_type=jnp.float32)
    prod_im = prod_im + jnp.einsum("eij,ejk->eik", green_im, sig_re, preferred_element_type=jnp.float32)
    prod_re = prod_re.astype(jnp.bfloat16)
    prod_im = prod_im.astype(jnp.bfloat16)
    real_part = jnp.einsum("eik,elk->eil", prod_re, green_re, preferred_element_type=jnp.float32)
    real_part = real_part + jnp.einsum("eik,elk->eil", prod_im, green_im, preferred_element_type=jnp.float32)
    imag_part = jnp.einsum("eik,elk->eil", prod_im, green_re, preferred_element_type=jnp.float32)
    imag_part = imag_part - jnp.einsum("eik,elk->eil", prod_re, green_im, preferred_element_type=jnp.float32)
    result = jnp.stack([real_part, imag_part], axis=1).astype(jnp.bfloat16)
    return result[None, :, None]


def solution(mesh):
    placed = (
        P("kz", "energy", None, None, None, None),
        P("kz", "energy", None, None, None, None, None),
        P(),
        P(),
        P(),
        P(),
        P(),
    )
    return jax.shard_map(
        per_device,
        mesh=mesh,
        in_specs=placed,
        out_specs=P("kz", "energy", None, None, None, None),
        check_vma=False,
    )
```

```python
import jax
import jax.numpy as jnp
from jax import lax
from jax.experimental import pallas as pl
from jax.experimental.pallas import tpu as pltpu
from jax.sharding import PartitionSpec as P

ORB = 4
NMODE = 2
ZHI = 4


def masks(neighbors, width):
    atoms = width // ORB
    own = jnp.arange(atoms, dtype=jnp.int32)[:, None]
    pairs = jnp.concatenate([own, neighbors[0]], axis=1)
    row_pairs = jnp.repeat(pairs, ORB, axis=0)
    col_atom = jnp.arange(width, dtype=jnp.int32) // ORB
    return (row_pairs.T[:, :, None] == col_atom[None, None, :]).astype(jnp.bfloat16)


def spread(width):
    return (jnp.arange(width)[:, None] % ORB == jnp.arange(ORB)[None, :]).astype(jnp.bfloat16)


def born_kernel(own_ref, q_ref, c_ref, occ_ref, sh_ref, out_ref, land, landf, part, relay_r, relay_l,
                near_r, near_l, far_r, far_l, sum_r, sum_l, gsend, grecv, send, recv):
    kz = lax.axis_index("kz")
    eb = lax.axis_index("energy")
    ne = lax.axis_size("energy")
    momenta = lax.axis_size("kz")
    xs = momenta // ZHI
    x = kz // ZHI
    h = kz % ZHI
    edev = own_ref.shape[0]
    rows = own_ref.shape[1]
    mesh = pl.DeviceIdType.MESH
    peers = [(d, t) for d in range(xs) for t in (-1, 0, 1) if (d, t) != (0, 0)]
    right = x * ZHI + (h + 1) % ZHI
    left = x * ZHI + (h + ZHI - 1) % ZHI

    def where(d, t):
        return {"kz": ((x + d) % xs) * ZHI + h, "energy": (eb + t + ne) % ne}

    barrier = pltpu.get_barrier_semaphore()
    for d, t in peers:
        pl.semaphore_signal(barrier, 1, device_id=where(d, t), device_id_type=mesh)
    for nb in (left, right):
        pl.semaphore_signal(barrier, 1, device_id={"kz": nb}, device_id_type=mesh)
    pl.semaphore_wait(barrier, len(peers) + 2)

    copies = []
    for i, (d, t) in enumerate(peers):
        c = pltpu.make_async_remote_copy(
            src_ref=own_ref, dst_ref=land.at[d, pl.ds((1 - t) * edev, edev)],
            send_sem=gsend.at[i], recv_sem=grecv.at[i], device_id=where(d, t), device_id_type=mesh,
        )
        c.start()
        copies.append(c)
    for e in range(edev):
        landf[0, edev + e] = own_ref[e].astype(jnp.float32)
    for c in copies:
        c.wait()
    keep = (jnp.where(eb > 0, 1.0, 0.0), 1.0, jnp.where(eb < ne - 1, 1.0, 0.0))
    for d in range(xs):
        for side in range(3):
            if (d, side) == (0, 1):
                continue
            for e in range(edev):
                landf[d, side * edev + e] = land[d, side * edev + e].astype(jnp.float32) * keep[side]

    shifts = [sh_ref[m] for m in range(NMODE)]

    def partial(z):
        k = x * ZHI + (h + z) % ZHI
        weights = []
        for d in range(xs):
            q = q_ref[k, ((x - d + xs) % xs) * ZHI + h]
            for m in range(NMODE):
                w = c_ref[m, q] / momenta
                weights.append((d, m, w * occ_ref[m], w * (occ_ref[m] + 1.0)))
        for e in range(edev):
            acc = jnp.zeros(own_ref.shape[1:], jnp.float32)
            for d, m, wl, wu in weights:
                acc = acc + wl * landf[d, edev + e - shifts[m]]
                acc = acc + wu * landf[d, edev + e + shifts[m]]
            part[z, pl.ds(e * rows, rows)] = acc

    def remote(src, dst, slot, to):
        return pltpu.make_async_remote_copy(
            src_ref=src, dst_ref=dst, send_sem=send.at[slot], recv_sem=recv.at[slot],
            device_id={"kz": to}, device_id_type=mesh,
        )

    total = part.shape[1]
    split = relay_r.shape[0]
    step = split // 2
    chunks_r = [(0, step), (step, split - step)]
    chunks_l = [(0, step), (step, total - split - step)]
    partial(2)
    far_right = [remote(part.at[2, pl.ds(o, n)], relay_r.at[pl.ds(o, n)], i, right)
                 for i, (o, n) in enumerate(chunks_r)]
    far_left = [remote(part.at[2, pl.ds(split + o, n)], relay_l.at[pl.ds(o, n)], 2 + i, left)
                for i, (o, n) in enumerate(chunks_l)]
    for c in far_right + far_left:
        c.start()
    partial(1)
    plain_right = remote(part.at[1, pl.ds(split, total - split)], near_r, 4, right)
    plain_right.start()
    partial(ZHI - 1)
    plain_left = remote(part.at[ZHI - 1, pl.ds(0, split)], near_l, 5, left)
    plain_left.start()
    partial(0)
    merged = []
    for i in range(2):
        o, n = chunks_r[i]
        far_right[i].wait_recv()
        sum_r[pl.ds(o, n)] = relay_r[pl.ds(o, n)] + part[1, pl.ds(o, n)]
        c = remote(sum_r.at[pl.ds(o, n)], far_r.at[pl.ds(o, n)], 6 + i, right)
        c.start()
        merged.append(c)
        o, n = chunks_l[i]
        far_left[i].wait_recv()
        sum_l[pl.ds(o, n)] = relay_l[pl.ds(o, n)] + part[ZHI - 1, pl.ds(split + o, n)]
        c = remote(sum_l.at[pl.ds(o, n)], far_l.at[pl.ds(o, n)], 8 + i, left)
        c.start()
        merged.append(c)
    plain_right.wait()
    plain_left.wait()
    for c in far_right + far_left:
        c.wait_send()
    for c in merged:
        c.wait()
    lo = pl.ds(0, split)
    hi = pl.ds(split, total - split)
    out_ref[lo] = (part[0, lo] + near_l[...] + far_r[...]).astype(out_ref.dtype)
    out_ref[hi] = (part[0, hi] + near_r[...] + far_l[...]).astype(out_ref.dtype)


def born(own, q_table, coupling, occupation, ph_shift):
    edev, rows, lanes = own.shape
    xs = lax.axis_size("kz") // ZHI
    total = edev * rows
    split = (total // 2 + 15) // 16 * 16
    vmem = pltpu.VMEM
    smem = pl.BlockSpec(memory_space=pltpu.SMEM)
    f32 = jnp.float32
    return pl.pallas_call(
        born_kernel,
        out_shape=jax.ShapeDtypeStruct((total, lanes), jnp.bfloat16),
        in_specs=[pl.BlockSpec(memory_space=vmem), smem, smem, smem, smem],
        out_specs=pl.BlockSpec(memory_space=vmem),
        scratch_shapes=[
            vmem((xs, 3 * edev, rows, lanes), own.dtype),
            vmem((xs, 3 * edev, rows, lanes), f32),
            vmem((ZHI, total, lanes), f32),
            vmem((split, lanes), f32),
            vmem((total - split, lanes), f32),
            vmem((total - split, lanes), f32),
            vmem((split, lanes), f32),
            vmem((split, lanes), f32),
            vmem((total - split, lanes), f32),
            vmem((split, lanes), f32),
            vmem((total - split, lanes), f32),
            pltpu.SemaphoreType.DMA((3 * xs - 1,)),
            pltpu.SemaphoreType.DMA((3 * xs - 1,)),
            pltpu.SemaphoreType.DMA((10,)),
            pltpu.SemaphoreType.DMA((10,)),
        ],
        compiler_params=pltpu.CompilerParams(collective_id=0, has_side_effects=True),
    )(own, q_table, coupling, occupation, ph_shift)


def keldysh_kernel(sig_ref, green_ref, sel_ref, maskt_ref, out_ref):
    f32 = jnp.float32
    edev = green_ref.shape[0]
    rows = sig_ref.shape[0] // edev
    members = maskt_ref.shape[0]

    def nt(a, b):
        return lax.dot_general(a, b, (((1,), (1,)), ((), ())), preferred_element_type=f32)

    for e in range(edev):
        sig = sig_ref[pl.ds(e * rows, rows), :]
        dense_t = []
        for n in range(2):
            acc = jnp.zeros(green_ref.shape[2:], f32)
            for j in range(members):
                tiled = jnp.dot(sel_ref[n * members + j], sig, preferred_element_type=f32)
                acc = acc + tiled * maskt_ref[j].astype(f32)
            dense_t.append(acc.astype(sig.dtype))
        gr = green_ref[e, 0]
        gi = green_ref[e, 1]
        pr = (nt(gr, dense_t[0]) - nt(gi, dense_t[1])).astype(gr.dtype)
        pi = (nt(gr, dense_t[1]) + nt(gi, dense_t[0])).astype(gr.dtype)
        out_ref[e, 0] = (nt(pr, gr) + nt(pi, gi)).astype(out_ref.dtype)
        out_ref[e, 1] = (nt(pi, gr) - nt(pr, gi)).astype(out_ref.dtype)


def keldysh(sigma, green, sel, maskt):
    vmem = pl.BlockSpec(memory_space=pltpu.VMEM)
    return pl.pallas_call(
        keldysh_kernel,
        out_shape=jax.ShapeDtypeStruct(green.shape, jnp.bfloat16),
        in_specs=[vmem, vmem, vmem, vmem],
        out_specs=vmem,
    )(sigma, green, sel, maskt)


def per_device(g_less, g_ret, neighbors, ph_shift, q_table, coupling, occupation):
    edev = g_less.shape[1]
    width = g_less.shape[4]
    members = neighbors.shape[2] + 1
    momenta = lax.axis_size("kz")
    xs = momenta // ZHI
    mask = masks(neighbors, width)
    e4 = spread(width)

    green = g_less[0, :, 0]
    held = green[:, :, None] * mask[None, None]
    picked = jnp.einsum("enjrc,cp->enjpr", held, e4, preferred_element_type=jnp.float32)
    picked = picked.astype(jnp.bfloat16).reshape(edev, 2 * members * ORB, width)
    sigma = born(picked, q_table, coupling, occupation, ph_shift)

    row = jnp.arange(2 * members * ORB)[None, :]
    col = jnp.arange(width)[:, None]
    sel = jnp.stack([
        (row // (members * ORB) == n) & ((row // ORB) % members == j) & (row % ORB == col % ORB)
        for n in range(2) for j in range(members)
    ]).astype(jnp.bfloat16)
    maskt = jnp.swapaxes(mask, 1, 2)
    result = keldysh(sigma, g_ret[0, :, 0, 0], sel, maskt)
    return result[None, :, None]


def solution(mesh):
    placed = (
        P("kz", "energy", None, None, None, None),
        P("kz", "energy", None, None, None, None, None),
        P(),
        P(),
        P(),
        P(),
        P(),
    )
    return jax.shard_map(
        per_device,
        mesh=mesh,
        in_specs=placed,
        out_specs=P("kz", "energy", None, None, None, None),
        check_vma=False,
    )
```

```python
import jax
import jax.numpy as jnp
from jax import lax
from jax.experimental import pallas as pl
from jax.experimental.pallas import tpu as pltpu
from jax.sharding import PartitionSpec as P

ORB = 4
NMODE = 2
ZHI = 4


def masks(neighbors, width):
    atoms = width // ORB
    own = jnp.arange(atoms, dtype=jnp.int32)[:, None]
    pairs = jnp.concatenate([own, neighbors[0]], axis=1)
    row_pairs = jnp.repeat(pairs, ORB, axis=0)
    col_atom = jnp.arange(width, dtype=jnp.int32) // ORB
    return (row_pairs.T[:, :, None] == col_atom[None, None, :]).astype(jnp.bfloat16)


def spread(width):
    return (jnp.arange(width)[:, None] % ORB == jnp.arange(ORB)[None, :]).astype(jnp.bfloat16)


def born_kernel(own_ref, q_ref, c_ref, occ_ref, sh_ref, out_ref, land, landf, part, relay_r, relay_l,
                near_r, near_l, far_r, far_l, sum_r, sum_l, gsend, grecv, send, recv):
    kz = lax.axis_index("kz")
    eb = lax.axis_index("energy")
    ne = lax.axis_size("energy")
    momenta = lax.axis_size("kz")
    xs = momenta // ZHI
    x = kz // ZHI
    h = kz % ZHI
    edev = own_ref.shape[0]
    rows = own_ref.shape[1]
    mesh = pl.DeviceIdType.MESH
    peers = [(d, t) for d in range(xs) for t in (-1, 0, 1) if (d, t) != (0, 0)]
    right = x * ZHI + (h + 1) % ZHI
    left = x * ZHI + (h + ZHI - 1) % ZHI

    def where(d, t):
        return {"kz": ((x + d) % xs) * ZHI + h, "energy": (eb + t + ne) % ne}

    barrier = pltpu.get_barrier_semaphore()
    for d, t in peers:
        pl.semaphore_signal(barrier, 1, device_id=where(d, t), device_id_type=mesh)
    for nb in (left, right):
        pl.semaphore_signal(barrier, 1, device_id={"kz": nb}, device_id_type=mesh)
    pl.semaphore_wait(barrier, len(peers) + 2)

    copies = []
    for i, (d, t) in enumerate(peers):
        c = pltpu.make_async_remote_copy(
            src_ref=own_ref, dst_ref=land.at[d, pl.ds((1 - t) * edev, edev)],
            send_sem=gsend.at[i], recv_sem=grecv.at[i], device_id=where(d, t), device_id_type=mesh,
        )
        c.start()
        copies.append(c)
    for e in range(edev):
        landf[0, edev + e] = own_ref[e].astype(jnp.float32)
    for c in copies:
        c.wait()
    keep = (jnp.where(eb > 0, 1.0, 0.0), 1.0, jnp.where(eb < ne - 1, 1.0, 0.0))
    for d in range(xs):
        for side in range(3):
            if (d, side) == (0, 1):
                continue
            for e in range(edev):
                landf[d, side * edev + e] = land[d, side * edev + e].astype(jnp.float32) * keep[side]

    shifts = [sh_ref[m] for m in range(NMODE)]

    def partial(z):
        k = x * ZHI + (h + z) % ZHI
        weights = []
        for d in range(xs):
            q = q_ref[k, ((x - d + xs) % xs) * ZHI + h]
            for m in range(NMODE):
                w = c_ref[m, q] / momenta
                weights.append((d, m, w * occ_ref[m], w * (occ_ref[m] + 1.0)))
        for e in range(edev):
            acc = jnp.zeros(own_ref.shape[1:], jnp.float32)
            for d, m, wl, wu in weights:
                acc = acc + wl * landf[d, edev + e - shifts[m]]
                acc = acc + wu * landf[d, edev + e + shifts[m]]
            part[z, pl.ds(e * rows, rows)] = acc

    def remote(src, dst, slot, to):
        return pltpu.make_async_remote_copy(
            src_ref=src, dst_ref=dst, send_sem=send.at[slot], recv_sem=recv.at[slot],
            device_id={"kz": to}, device_id_type=mesh,
        )

    total = part.shape[1]
    split = relay_r.shape[0]
    step = split // 2
    chunks_r = [(0, step), (step, split - step)]
    chunks_l = [(0, step), (step, total - split - step)]
    partial(2)
    far_right = [remote(part.at[2, pl.ds(o, n)], relay_r.at[pl.ds(o, n)], i, right)
                 for i, (o, n) in enumerate(chunks_r)]
    far_left = [remote(part.at[2, pl.ds(split + o, n)], relay_l.at[pl.ds(o, n)], 2 + i, left)
                for i, (o, n) in enumerate(chunks_l)]
    for c in far_right + far_left:
        c.start()
    partial(1)
    plain_right = remote(part.at[1, pl.ds(split, total - split)], near_r, 4, right)
    plain_right.start()
    partial(ZHI - 1)
    plain_left = remote(part.at[ZHI - 1, pl.ds(0, split)], near_l, 5, left)
    plain_left.start()
    partial(0)
    merged = []
    for i in range(2):
        o, n = chunks_r[i]
        far_right[i].wait_recv()
        sum_r[pl.ds(o, n)] = relay_r[pl.ds(o, n)] + part[1, pl.ds(o, n)]
        c = remote(sum_r.at[pl.ds(o, n)], far_r.at[pl.ds(o, n)], 6 + i, right)
        c.start()
        merged.append(c)
        o, n = chunks_l[i]
        far_left[i].wait_recv()
        sum_l[pl.ds(o, n)] = relay_l[pl.ds(o, n)] + part[ZHI - 1, pl.ds(split + o, n)]
        c = remote(sum_l.at[pl.ds(o, n)], far_l.at[pl.ds(o, n)], 8 + i, left)
        c.start()
        merged.append(c)
    plain_right.wait()
    plain_left.wait()
    for c in far_right + far_left:
        c.wait_send()
    for c in merged:
        c.wait()
    lo = pl.ds(0, split)
    hi = pl.ds(split, total - split)
    out_ref[lo] = (part[0, lo] + near_l[...] + far_r[...]).astype(out_ref.dtype)
    out_ref[hi] = (part[0, hi] + near_r[...] + far_l[...]).astype(out_ref.dtype)


def born(own, q_table, coupling, occupation, ph_shift):
    edev, rows, lanes = own.shape
    xs = lax.axis_size("kz") // ZHI
    total = edev * rows
    split = (total // 2 + 15) // 16 * 16
    vmem = pltpu.VMEM
    smem = pl.BlockSpec(memory_space=pltpu.SMEM)
    f32 = jnp.float32
    return pl.pallas_call(
        born_kernel,
        out_shape=jax.ShapeDtypeStruct((total, lanes), jnp.bfloat16),
        in_specs=[pl.BlockSpec(memory_space=vmem), smem, smem, smem, smem],
        out_specs=pl.BlockSpec(memory_space=vmem),
        scratch_shapes=[
            vmem((xs, 3 * edev, rows, lanes), own.dtype),
            vmem((xs, 3 * edev, rows, lanes), f32),
            vmem((ZHI, total, lanes), f32),
            vmem((split, lanes), f32),
            vmem((total - split, lanes), f32),
            vmem((total - split, lanes), f32),
            vmem((split, lanes), f32),
            vmem((split, lanes), f32),
            vmem((total - split, lanes), f32),
            vmem((split, lanes), f32),
            vmem((total - split, lanes), f32),
            pltpu.SemaphoreType.DMA((3 * xs - 1,)),
            pltpu.SemaphoreType.DMA((3 * xs - 1,)),
            pltpu.SemaphoreType.DMA((10,)),
            pltpu.SemaphoreType.DMA((10,)),
        ],
        compiler_params=pltpu.CompilerParams(collective_id=0, has_side_effects=True),
    )(own, q_table, coupling, occupation, ph_shift)


def keldysh_kernel(sig_ref, green_ref, maskt_ref, out_ref):
    f32 = jnp.float32
    edev = green_ref.shape[0]
    rows = sig_ref.shape[0] // edev
    members = maskt_ref.shape[0]
    width = green_ref.shape[2]
    lane = lax.broadcasted_iota(jnp.int32, (width, rows), 1)
    spread = lax.broadcasted_iota(jnp.int32, (width, rows), 0) & (ORB - 1)

    def sel(base):
        return jnp.where(lane - base == spread, 1.0, 0.0).astype(sig_ref.dtype)

    def nt(a, b):
        return lax.dot_general(a, b, (((1,), (1,)), ((), ())), preferred_element_type=f32)

    for e in range(edev):
        sig = sig_ref[pl.ds(e * rows, rows), :]
        dense_t = []
        for n in range(2):
            acc = jnp.zeros(green_ref.shape[2:], f32)
            for j in range(members):
                tiled = jnp.dot(sel((n * members + j) * ORB), sig, preferred_element_type=f32)
                acc = acc + tiled * maskt_ref[j].astype(f32)
            dense_t.append(acc.astype(sig.dtype))
        gr = green_ref[e, 0]
        gi = green_ref[e, 1]
        pr = (nt(gr, dense_t[0]) - nt(gi, dense_t[1])).astype(gr.dtype)
        pi = (nt(gr, dense_t[1]) + nt(gi, dense_t[0])).astype(gr.dtype)
        out_ref[e, 0] = (nt(pr, gr) + nt(pi, gi)).astype(out_ref.dtype)
        out_ref[e, 1] = (nt(pi, gr) - nt(pr, gi)).astype(out_ref.dtype)


def keldysh(sigma, green, maskt):
    vmem = pl.BlockSpec(memory_space=pltpu.VMEM)
    return pl.pallas_call(
        keldysh_kernel,
        out_shape=jax.ShapeDtypeStruct(green.shape, jnp.bfloat16),
        in_specs=[vmem, vmem, vmem],
        out_specs=vmem,
    )(sigma, green, maskt)


def per_device(g_less, g_ret, neighbors, ph_shift, q_table, coupling, occupation):
    edev = g_less.shape[1]
    width = g_less.shape[4]
    members = neighbors.shape[2] + 1
    momenta = lax.axis_size("kz")
    xs = momenta // ZHI
    mask = masks(neighbors, width)
    e4 = spread(width)

    green = g_less[0, :, 0]
    held = green[:, :, None] * mask[None, None]
    picked = jnp.einsum("enjrc,cp->enjpr", held, e4, preferred_element_type=jnp.float32)
    picked = picked.astype(jnp.bfloat16).reshape(edev, 2 * members * ORB, width)
    sigma = born(picked, q_table, coupling, occupation, ph_shift)

    sigma, later = lax.optimization_barrier((sigma, neighbors))
    maskt = jnp.swapaxes(masks(later, width), 1, 2)
    result = keldysh(sigma, g_ret[0, :, 0, 0], maskt)
    return result[None, :, None]


def solution(mesh):
    placed = (
        P("kz", "energy", None, None, None, None),
        P("kz", "energy", None, None, None, None, None),
        P(),
        P(),
        P(),
        P(),
        P(),
    )
    return jax.shard_map(
        per_device,
        mesh=mesh,
        in_specs=placed,
        out_specs=P("kz", "energy", None, None, None, None),
        check_vma=False,
    )
```

```python
import jax
import jax.numpy as jnp
from jax import lax
from jax.experimental import pallas as pl
from jax.experimental.pallas import tpu as pltpu
from jax.sharding import PartitionSpec as P

ORB = 4
NMODE = 2
ZHI = 4


def masks(neighbors, width):
    atoms = width // ORB
    own = jnp.arange(atoms, dtype=jnp.int32)[:, None]
    pairs = jnp.concatenate([own, neighbors[0]], axis=1)
    row_pairs = jnp.repeat(pairs, ORB, axis=0)
    col_atom = jnp.arange(width, dtype=jnp.int32) // ORB
    return (row_pairs.T[:, :, None] == col_atom[None, None, :]).astype(jnp.bfloat16)


def born_kernel(g_ref, mask_ref, q_ref, c_ref, occ_ref, sh_ref, out_ref, own_ref, land, landf, part, relay_r,
                relay_l, near_r, near_l, far_r, far_l, sum_r, sum_l, gsend, grecv, send, recv):
    kz = lax.axis_index("kz")
    eb = lax.axis_index("energy")
    ne = lax.axis_size("energy")
    momenta = lax.axis_size("kz")
    xs = momenta // ZHI
    x = kz // ZHI
    h = kz % ZHI
    edev = own_ref.shape[0]
    rows = own_ref.shape[1]
    mesh = pl.DeviceIdType.MESH
    peers = [(d, t) for d in range(xs) for t in (-1, 0, 1) if (d, t) != (0, 0)]
    right = x * ZHI + (h + 1) % ZHI
    left = x * ZHI + (h + ZHI - 1) % ZHI

    def where(d, t):
        return {"kz": ((x + d) % xs) * ZHI + h, "energy": (eb + t + ne) % ne}

    barrier = pltpu.get_barrier_semaphore()
    for d, t in peers:
        pl.semaphore_signal(barrier, 1, device_id=where(d, t), device_id_type=mesh)
    for nb in (left, right):
        pl.semaphore_signal(barrier, 1, device_id={"kz": nb}, device_id_type=mesh)

    members = mask_ref.shape[0]
    width = g_ref.shape[2]
    line = lax.broadcasted_iota(jnp.int32, (rows, width), 0)
    spread = lax.broadcasted_iota(jnp.int32, (rows, width), 1) & (ORB - 1)
    for e in range(edev):
        acc = jnp.zeros((rows, width), jnp.float32)
        for n in range(2):
            green = g_ref[e, n]
            for j in range(members):
                sel_t = jnp.where(line - (n * members + j) * ORB == spread, 1.0, 0.0).astype(green.dtype)
                held = green * mask_ref[j]
                acc = acc + lax.dot_general(
                    sel_t, held, (((1,), (1,)), ((), ())), preferred_element_type=jnp.float32
                )
        own_ref[e] = acc.astype(own_ref.dtype)
        landf[0, edev + e] = acc
    pl.semaphore_wait(barrier, len(peers) + 2)

    copies = []
    for i, (d, t) in enumerate(peers):
        c = pltpu.make_async_remote_copy(
            src_ref=own_ref, dst_ref=land.at[d, pl.ds((1 - t) * edev, edev)],
            send_sem=gsend.at[i], recv_sem=grecv.at[i], device_id=where(d, t), device_id_type=mesh,
        )
        c.start()
        copies.append(c)
    for c in copies:
        c.wait()
    keep = (jnp.where(eb > 0, 1.0, 0.0), 1.0, jnp.where(eb < ne - 1, 1.0, 0.0))
    for d in range(xs):
        for side in range(3):
            if (d, side) == (0, 1):
                continue
            for e in range(edev):
                landf[d, side * edev + e] = land[d, side * edev + e].astype(jnp.float32) * keep[side]

    shifts = [sh_ref[m] for m in range(NMODE)]

    def partial(z):
        k = x * ZHI + (h + z) % ZHI
        weights = []
        for d in range(xs):
            q = q_ref[k, ((x - d + xs) % xs) * ZHI + h]
            for m in range(NMODE):
                w = c_ref[m, q] / momenta
                weights.append((d, m, w * occ_ref[m], w * (occ_ref[m] + 1.0)))
        for e in range(edev):
            acc = jnp.zeros(own_ref.shape[1:], jnp.float32)
            for d, m, wl, wu in weights:
                acc = acc + wl * landf[d, edev + e - shifts[m]]
                acc = acc + wu * landf[d, edev + e + shifts[m]]
            part[z, pl.ds(e * rows, rows)] = acc

    def remote(src, dst, slot, to):
        return pltpu.make_async_remote_copy(
            src_ref=src, dst_ref=dst, send_sem=send.at[slot], recv_sem=recv.at[slot],
            device_id={"kz": to}, device_id_type=mesh,
        )

    total = part.shape[1]
    split = relay_r.shape[0]
    step = split // 2
    chunks_r = [(0, step), (step, split - step)]
    chunks_l = [(0, step), (step, total - split - step)]
    partial(2)
    far_right = [remote(part.at[2, pl.ds(o, n)], relay_r.at[pl.ds(o, n)], i, right)
                 for i, (o, n) in enumerate(chunks_r)]
    far_left = [remote(part.at[2, pl.ds(split + o, n)], relay_l.at[pl.ds(o, n)], 2 + i, left)
                for i, (o, n) in enumerate(chunks_l)]
    for c in far_right + far_left:
        c.start()
    partial(1)
    plain_right = remote(part.at[1, pl.ds(split, total - split)], near_r, 4, right)
    plain_right.start()
    partial(ZHI - 1)
    plain_left = remote(part.at[ZHI - 1, pl.ds(0, split)], near_l, 5, left)
    plain_left.start()
    partial(0)
    merged = []
    for i in range(2):
        o, n = chunks_r[i]
        far_right[i].wait_recv()
        sum_r[pl.ds(o, n)] = relay_r[pl.ds(o, n)] + part[1, pl.ds(o, n)]
        c = remote(sum_r.at[pl.ds(o, n)], far_r.at[pl.ds(o, n)], 6 + i, right)
        c.start()
        merged.append(c)
        o, n = chunks_l[i]
        far_left[i].wait_recv()
        sum_l[pl.ds(o, n)] = relay_l[pl.ds(o, n)] + part[ZHI - 1, pl.ds(split + o, n)]
        c = remote(sum_l.at[pl.ds(o, n)], far_l.at[pl.ds(o, n)], 8 + i, left)
        c.start()
        merged.append(c)
    plain_right.wait()
    plain_left.wait()
    for c in far_right + far_left:
        c.wait_send()
    for c in merged:
        c.wait()
    lo = pl.ds(0, split)
    hi = pl.ds(split, total - split)
    out_ref[lo] = (part[0, lo] + near_l[...] + far_r[...]).astype(out_ref.dtype)
    out_ref[hi] = (part[0, hi] + near_r[...] + far_l[...]).astype(out_ref.dtype)


def born(green, mask, q_table, coupling, occupation, ph_shift):
    edev = green.shape[0]
    lanes = green.shape[3]
    rows = 2 * mask.shape[0] * ORB
    xs = lax.axis_size("kz") // ZHI
    total = edev * rows
    split = (total // 2 + 15) // 16 * 16
    vmem = pltpu.VMEM
    smem = pl.BlockSpec(memory_space=pltpu.SMEM)
    f32 = jnp.float32
    return pl.pallas_call(
        born_kernel,
        out_shape=jax.ShapeDtypeStruct((total, lanes), jnp.bfloat16),
        in_specs=[pl.BlockSpec(memory_space=vmem), pl.BlockSpec(memory_space=vmem), smem, smem, smem, smem],
        out_specs=pl.BlockSpec(memory_space=vmem),
        scratch_shapes=[
            vmem((edev, rows, lanes), green.dtype),
            vmem((xs, 3 * edev, rows, lanes), green.dtype),
            vmem((xs, 3 * edev, rows, lanes), f32),
            vmem((ZHI, total, lanes), f32),
            vmem((split, lanes), f32),
            vmem((total - split, lanes), f32),
            vmem((total - split, lanes), f32),
            vmem((split, lanes), f32),
            vmem((split, lanes), f32),
            vmem((total - split, lanes), f32),
            vmem((split, lanes), f32),
            vmem((total - split, lanes), f32),
            pltpu.SemaphoreType.DMA((3 * xs - 1,)),
            pltpu.SemaphoreType.DMA((3 * xs - 1,)),
            pltpu.SemaphoreType.DMA((10,)),
            pltpu.SemaphoreType.DMA((10,)),
        ],
        compiler_params=pltpu.CompilerParams(collective_id=0, has_side_effects=True),
    )(green, mask, q_table, coupling, occupation, ph_shift)


def keldysh_kernel(sig_ref, green_ref, mask_ref, out_ref):
    f32 = jnp.float32
    edev = green_ref.shape[0]
    rows = sig_ref.shape[0] // edev
    members = mask_ref.shape[0]
    width = green_ref.shape[2]
    mask_t = [mask_ref[j].astype(f32).T for j in range(members)]
    lane = lax.broadcasted_iota(jnp.int32, (width, rows), 1)
    spread = lax.broadcasted_iota(jnp.int32, (width, rows), 0) & (ORB - 1)

    def sel(base):
        return jnp.where(lane - base == spread, 1.0, 0.0).astype(sig_ref.dtype)

    def nt(a, b):
        return lax.dot_general(a, b, (((1,), (1,)), ((), ())), preferred_element_type=f32)

    for e in range(edev):
        sig = sig_ref[pl.ds(e * rows, rows), :]
        dense_t = []
        for n in range(2):
            acc = jnp.zeros(green_ref.shape[2:], f32)
            for j in range(members):
                tiled = jnp.dot(sel((n * members + j) * ORB), sig, preferred_element_type=f32)
                acc = acc + tiled * mask_t[j]
            dense_t.append(acc.astype(sig.dtype))
        gr = green_ref[e, 0]
        gi = green_ref[e, 1]
        pr = (nt(gr, dense_t[0]) - nt(gi, dense_t[1])).astype(gr.dtype)
        pi = (nt(gr, dense_t[1]) + nt(gi, dense_t[0])).astype(gr.dtype)
        out_ref[e, 0] = (nt(pr, gr) + nt(pi, gi)).astype(out_ref.dtype)
        out_ref[e, 1] = (nt(pi, gr) - nt(pr, gi)).astype(out_ref.dtype)


def keldysh(sigma, green, mask):
    vmem = pl.BlockSpec(memory_space=pltpu.VMEM)
    return pl.pallas_call(
        keldysh_kernel,
        out_shape=jax.ShapeDtypeStruct(green.shape, jnp.bfloat16),
        in_specs=[vmem, vmem, vmem],
        out_specs=vmem,
    )(sigma, green, mask)


def per_device(g_less, g_ret, neighbors, ph_shift, q_table, coupling, occupation):
    width = g_less.shape[4]
    mask = masks(neighbors, width)
    sigma = born(g_less[0, :, 0], mask, q_table, coupling, occupation, ph_shift)
    result = keldysh(sigma, g_ret[0, :, 0, 0], mask)
    return result[None, :, None]


def solution(mesh):
    placed = (
        P("kz", "energy", None, None, None, None),
        P("kz", "energy", None, None, None, None, None),
        P(),
        P(),
        P(),
        P(),
        P(),
    )
    return jax.shard_map(
        per_device,
        mesh=mesh,
        in_specs=placed,
        out_specs=P("kz", "energy", None, None, None, None),
        check_vma=False,
    )
```

```python
import jax
import jax.numpy as jnp
from jax import lax
from jax.experimental import pallas as pl
from jax.experimental.pallas import tpu as pltpu
from jax.sharding import PartitionSpec as P

ORB = 4
NMODE = 2
ZHI = 4


def masks(neighbors, width):
    atoms = width // ORB
    own = jnp.arange(atoms, dtype=jnp.int32)[:, None]
    pairs = jnp.concatenate([own, neighbors[0]], axis=1)
    row_pairs = jnp.repeat(pairs, ORB, axis=0)
    col_atom = jnp.arange(width, dtype=jnp.int32) // ORB
    return (row_pairs.T[:, :, None] == col_atom[None, None, :]).astype(jnp.bfloat16)


def born_kernel(g_ref, mask_ref, q_ref, c_ref, occ_ref, sh_ref, out_ref, own_ref, land, landf, part, relay_r,
                relay_l, near_r, near_l, far_r, far_l, sum_r, sum_l, gsend, grecv, send, recv):
    kz = lax.axis_index("kz")
    eb = lax.axis_index("energy")
    ne = lax.axis_size("energy")
    momenta = lax.axis_size("kz")
    xs = momenta // ZHI
    x = kz // ZHI
    h = kz % ZHI
    edev = own_ref.shape[0]
    rows = own_ref.shape[1]
    mesh = pl.DeviceIdType.MESH
    peers = [(d, t) for d in range(xs) for t in (-1, 0, 1) if (d, t) != (0, 0)]
    right = x * ZHI + (h + 1) % ZHI
    left = x * ZHI + (h + ZHI - 1) % ZHI

    def where(d, t):
        return {"kz": ((x + d) % xs) * ZHI + h, "energy": (eb + t + ne) % ne}

    barrier = pltpu.get_barrier_semaphore()
    for d, t in peers:
        pl.semaphore_signal(barrier, 1, device_id=where(d, t), device_id_type=mesh)
    for nb in (left, right):
        pl.semaphore_signal(barrier, 1, device_id={"kz": nb}, device_id_type=mesh)

    members = mask_ref.shape[0]
    width = g_ref.shape[2]
    line = lax.broadcasted_iota(jnp.int32, (rows, width), 0)
    spread = lax.broadcasted_iota(jnp.int32, (rows, width), 1) & (ORB - 1)
    for e in range(edev):
        acc = jnp.zeros((rows, width), jnp.float32)
        for n in range(2):
            green = g_ref[e, n]
            for j in range(members):
                sel_t = jnp.where(line - (n * members + j) * ORB == spread, 1.0, 0.0).astype(green.dtype)
                held = green * mask_ref[j]
                acc = acc + lax.dot_general(
                    sel_t, held, (((1,), (1,)), ((), ())), preferred_element_type=jnp.float32
                )
        own_ref[e] = acc.astype(own_ref.dtype)
        landf[0, edev + e] = acc
    pl.semaphore_wait(barrier, len(peers) + 2)

    copies = []
    for i, (d, t) in enumerate(peers):
        c = pltpu.make_async_remote_copy(
            src_ref=own_ref, dst_ref=land.at[d, pl.ds((1 - t) * edev, edev)],
            send_sem=gsend.at[i], recv_sem=grecv.at[i], device_id=where(d, t), device_id_type=mesh,
        )
        c.start()
        copies.append(c)
    for c in copies:
        c.wait()
    keep = (jnp.where(eb > 0, 1.0, 0.0), 1.0, jnp.where(eb < ne - 1, 1.0, 0.0))
    for d in range(xs):
        for side in range(3):
            if (d, side) == (0, 1):
                continue
            for e in range(edev):
                landf[d, side * edev + e] = land[d, side * edev + e].astype(jnp.float32) * keep[side]

    shifts = [sh_ref[m] for m in range(NMODE)]

    def partial(z):
        k = x * ZHI + (h + z) % ZHI
        weights = []
        for d in range(xs):
            q = q_ref[k, ((x - d + xs) % xs) * ZHI + h]
            for m in range(NMODE):
                w = c_ref[m, q] / momenta
                weights.append((d, m, w * occ_ref[m], w * (occ_ref[m] + 1.0)))
        for e in range(edev):
            acc = jnp.zeros(own_ref.shape[1:], jnp.float32)
            for d, m, wl, wu in weights:
                acc = acc + wl * landf[d, edev + e - shifts[m]]
                acc = acc + wu * landf[d, edev + e + shifts[m]]
            part[z, pl.ds(e * rows, rows)] = acc

    def remote(src, dst, slot, to):
        return pltpu.make_async_remote_copy(
            src_ref=src, dst_ref=dst, send_sem=send.at[slot], recv_sem=recv.at[slot],
            device_id={"kz": to}, device_id_type=mesh,
        )

    total = part.shape[1]
    split = relay_r.shape[0]
    step = split // 2
    chunks_r = [(0, step), (step, split - step)]
    chunks_l = [(0, step), (step, total - split - step)]
    partial(2)
    far_right = [remote(part.at[2, pl.ds(o, n)], relay_r.at[pl.ds(o, n)], i, right)
                 for i, (o, n) in enumerate(chunks_r)]
    far_left = [remote(part.at[2, pl.ds(split + o, n)], relay_l.at[pl.ds(o, n)], 2 + i, left)
                for i, (o, n) in enumerate(chunks_l)]
    for c in far_right + far_left:
        c.start()
    partial(1)
    plain_right = remote(part.at[1, pl.ds(split, total - split)], near_r, 4, right)
    plain_right.start()
    partial(ZHI - 1)
    plain_left = remote(part.at[ZHI - 1, pl.ds(0, split)], near_l, 5, left)
    plain_left.start()
    partial(0)
    merged = []
    for i in range(2):
        o, n = chunks_r[i]
        far_right[i].wait_recv()
        sum_r[pl.ds(o, n)] = relay_r[pl.ds(o, n)] + part[1, pl.ds(o, n)]
        c = remote(sum_r.at[pl.ds(o, n)], far_r.at[pl.ds(o, n)], 6 + i, right)
        c.start()
        merged.append(c)
        o, n = chunks_l[i]
        far_left[i].wait_recv()
        sum_l[pl.ds(o, n)] = relay_l[pl.ds(o, n)] + part[ZHI - 1, pl.ds(split + o, n)]
        c = remote(sum_l.at[pl.ds(o, n)], far_l.at[pl.ds(o, n)], 8 + i, left)
        c.start()
        merged.append(c)
    plain_right.wait()
    plain_left.wait()
    for c in far_right + far_left:
        c.wait_send()
    for c in merged:
        c.wait()
    lo = pl.ds(0, split)
    hi = pl.ds(split, total - split)
    out_ref[lo] = (part[0, lo] + near_l[...] + far_r[...]).astype(out_ref.dtype)
    out_ref[hi] = (part[0, hi] + near_r[...] + far_l[...]).astype(out_ref.dtype)


def born(green, mask, q_table, coupling, occupation, ph_shift):
    edev = green.shape[0]
    lanes = green.shape[3]
    rows = 2 * mask.shape[0] * ORB
    xs = lax.axis_size("kz") // ZHI
    total = edev * rows
    split = (total // 2 + 15) // 16 * 16
    vmem = pltpu.VMEM
    smem = pl.BlockSpec(memory_space=pltpu.SMEM)
    f32 = jnp.float32
    return pl.pallas_call(
        born_kernel,
        out_shape=jax.ShapeDtypeStruct((total, lanes), jnp.bfloat16),
        in_specs=[pl.BlockSpec(memory_space=vmem), pl.BlockSpec(memory_space=vmem), smem, smem, smem, smem],
        out_specs=pl.BlockSpec(memory_space=vmem),
        scratch_shapes=[
            vmem((edev, rows, lanes), green.dtype),
            vmem((xs, 3 * edev, rows, lanes), green.dtype),
            vmem((xs, 3 * edev, rows, lanes), f32),
            vmem((ZHI, total, lanes), f32),
            vmem((split, lanes), f32),
            vmem((total - split, lanes), f32),
            vmem((total - split, lanes), f32),
            vmem((split, lanes), f32),
            vmem((split, lanes), f32),
            vmem((total - split, lanes), f32),
            vmem((split, lanes), f32),
            vmem((total - split, lanes), f32),
            pltpu.SemaphoreType.DMA((3 * xs - 1,)),
            pltpu.SemaphoreType.DMA((3 * xs - 1,)),
            pltpu.SemaphoreType.DMA((10,)),
            pltpu.SemaphoreType.DMA((10,)),
        ],
        compiler_params=pltpu.CompilerParams(collective_id=0, has_side_effects=True),
    )(green, mask, q_table, coupling, occupation, ph_shift)


def keldysh_kernel(sig_ref, green_ref, mask_ref, out_ref):
    f32 = jnp.float32
    edev = green_ref.shape[0]
    rows = sig_ref.shape[0] // edev
    members = mask_ref.shape[0]
    width = green_ref.shape[2]
    mask_t = [mask_ref[j].astype(f32).T for j in range(members)]
    tall = lax.broadcasted_iota(jnp.int32, (members * width, rows), 0)
    lane = lax.broadcasted_iota(jnp.int32, (members * width, rows), 1)
    sel = [
        jnp.where(lane - n * members * ORB - ORB * (tall // width) == (tall & (ORB - 1)), 1.0, 0.0).astype(sig_ref.dtype)
        for n in range(2)
    ]

    def nt(a, b):
        return lax.dot_general(a, b, (((1,), (1,)), ((), ())), preferred_element_type=f32)

    for e in range(edev):
        sig = sig_ref[pl.ds(e * rows, rows), :]
        dense_t = []
        for n in range(2):
            tiled = jnp.dot(sel[n], sig, preferred_element_type=f32)
            acc = tiled[0:width] * mask_t[0]
            for j in range(1, members):
                acc = acc + tiled[j * width:(j + 1) * width] * mask_t[j]
            dense_t.append(acc.astype(sig.dtype))
        gr = green_ref[e, 0]
        gi = green_ref[e, 1]
        blocks = nt(jnp.concatenate([gr, gi], 0), jnp.concatenate(dense_t, 0))
        pr = (blocks[:width, :width] - blocks[width:, width:]).astype(gr.dtype)
        pi = (blocks[:width, width:] + blocks[width:, :width]).astype(gr.dtype)
        lhs = jnp.concatenate([jnp.concatenate([pr, pi], 1), jnp.concatenate([pi, -pr], 1)], 0)
        both = nt(lhs, jnp.concatenate([gr, gi], 1))
        out_ref[e, 0] = both[:width].astype(out_ref.dtype)
        out_ref[e, 1] = both[width:].astype(out_ref.dtype)


def keldysh(sigma, green, mask):
    vmem = pl.BlockSpec(memory_space=pltpu.VMEM)
    return pl.pallas_call(
        keldysh_kernel,
        out_shape=jax.ShapeDtypeStruct(green.shape, jnp.bfloat16),
        in_specs=[vmem, vmem, vmem],
        out_specs=vmem,
    )(sigma, green, mask)


def per_device(g_less, g_ret, neighbors, ph_shift, q_table, coupling, occupation):
    width = g_less.shape[4]
    mask = masks(neighbors, width)
    sigma = born(g_less[0, :, 0], mask, q_table, coupling, occupation, ph_shift)
    result = keldysh(sigma, g_ret[0, :, 0, 0], mask)
    return result[None, :, None]


def solution(mesh):
    placed = (
        P("kz", "energy", None, None, None, None),
        P("kz", "energy", None, None, None, None, None),
        P(),
        P(),
        P(),
        P(),
        P(),
    )
    return jax.shard_map(
        per_device,
        mesh=mesh,
        in_specs=placed,
        out_specs=P("kz", "energy", None, None, None, None),
        check_vma=False,
    )
```

```python
import jax
import jax.numpy as jnp
from jax import lax
from jax.experimental import pallas as pl
from jax.experimental.pallas import tpu as pltpu
from jax.sharding import PartitionSpec as P

ORB = 4
NMODE = 2
ZHI = 4


def masks(neighbors, width):
    atoms = width // ORB
    own = jnp.arange(atoms, dtype=jnp.int32)[:, None]
    pairs = jnp.concatenate([own, neighbors[0]], axis=1)
    row_pairs = jnp.repeat(pairs, ORB, axis=0)
    col_atom = jnp.arange(width, dtype=jnp.int32) // ORB
    return (row_pairs.T[:, :, None] == col_atom[None, None, :]).astype(jnp.bfloat16)


def born_kernel(g_hbm, mask_ref, q_ref, c_ref, occ_ref, sh_ref, out_ref, g_ref, g_sem, own_ref, land, landf, part,
                relay_r, relay_l, near_r, near_l, far_r, far_l, sum_r, sum_l, gsend, grecv, send, recv):
    kz = lax.axis_index("kz")
    eb = lax.axis_index("energy")
    ne = lax.axis_size("energy")
    momenta = lax.axis_size("kz")
    xs = momenta // ZHI
    x = kz // ZHI
    h = kz % ZHI
    edev = own_ref.shape[0]
    rows = own_ref.shape[1]
    mesh = pl.DeviceIdType.MESH
    peers = [(d, t) for d in range(xs) for t in (-1, 0, 1) if (d, t) != (0, 0)]
    right = x * ZHI + (h + 1) % ZHI
    left = x * ZHI + (h + ZHI - 1) % ZHI

    def where(d, t):
        return {"kz": ((x + d) % xs) * ZHI + h, "energy": (eb + t + ne) % ne}

    fetch = pltpu.make_async_copy(g_hbm, g_ref, g_sem)
    fetch.start()
    barrier = pltpu.get_barrier_semaphore()
    for d, t in peers:
        pl.semaphore_signal(barrier, 1, device_id=where(d, t), device_id_type=mesh)
    for nb in (left, right):
        pl.semaphore_signal(barrier, 1, device_id={"kz": nb}, device_id_type=mesh)
    fetch.wait()

    members = mask_ref.shape[0]
    width = g_ref.shape[2]
    line = lax.broadcasted_iota(jnp.int32, (rows, width), 0)
    spread = lax.broadcasted_iota(jnp.int32, (rows, width), 1) & (ORB - 1)
    for e in range(edev):
        acc = jnp.zeros((rows, width), jnp.float32)
        for n in range(2):
            green = g_ref[e, n]
            for j in range(members):
                sel_t = jnp.where(line - (n * members + j) * ORB == spread, 1.0, 0.0).astype(green.dtype)
                held = green * mask_ref[j]
                acc = acc + lax.dot_general(
                    sel_t, held, (((1,), (1,)), ((), ())), preferred_element_type=jnp.float32
                )
        own_ref[e] = acc.astype(own_ref.dtype)
        landf[0, edev + e] = acc
    pl.semaphore_wait(barrier, len(peers) + 2)

    copies = []
    for i, (d, t) in enumerate(peers):
        c = pltpu.make_async_remote_copy(
            src_ref=own_ref, dst_ref=land.at[d, pl.ds((1 - t) * edev, edev)],
            send_sem=gsend.at[i], recv_sem=grecv.at[i], device_id=where(d, t), device_id_type=mesh,
        )
        c.start()
        copies.append(c)
    for c in copies:
        c.wait()
    keep = (jnp.where(eb > 0, 1.0, 0.0), 1.0, jnp.where(eb < ne - 1, 1.0, 0.0))
    for d in range(xs):
        for side in range(3):
            if (d, side) == (0, 1):
                continue
            for e in range(edev):
                landf[d, side * edev + e] = land[d, side * edev + e].astype(jnp.float32) * keep[side]

    shifts = [sh_ref[m] for m in range(NMODE)]

    def partial(z):
        k = x * ZHI + (h + z) % ZHI
        weights = []
        for d in range(xs):
            q = q_ref[k, ((x - d + xs) % xs) * ZHI + h]
            for m in range(NMODE):
                w = c_ref[m, q] / momenta
                weights.append((d, m, w * occ_ref[m], w * (occ_ref[m] + 1.0)))
        for e in range(edev):
            acc = jnp.zeros(own_ref.shape[1:], jnp.float32)
            for d, m, wl, wu in weights:
                acc = acc + wl * landf[d, edev + e - shifts[m]]
                acc = acc + wu * landf[d, edev + e + shifts[m]]
            part[z, pl.ds(e * rows, rows)] = acc

    def remote(src, dst, slot, to):
        return pltpu.make_async_remote_copy(
            src_ref=src, dst_ref=dst, send_sem=send.at[slot], recv_sem=recv.at[slot],
            device_id={"kz": to}, device_id_type=mesh,
        )

    total = part.shape[1]
    split = relay_r.shape[0]
    step = split // 2
    chunks_r = [(0, step), (step, split - step)]
    chunks_l = [(0, step), (step, total - split - step)]
    partial(2)
    far_right = [remote(part.at[2, pl.ds(o, n)], relay_r.at[pl.ds(o, n)], i, right)
                 for i, (o, n) in enumerate(chunks_r)]
    far_left = [remote(part.at[2, pl.ds(split + o, n)], relay_l.at[pl.ds(o, n)], 2 + i, left)
                for i, (o, n) in enumerate(chunks_l)]
    for c in far_right + far_left:
        c.start()
    partial(1)
    plain_right = remote(part.at[1, pl.ds(split, total - split)], near_r, 4, right)
    plain_right.start()
    partial(ZHI - 1)
    plain_left = remote(part.at[ZHI - 1, pl.ds(0, split)], near_l, 5, left)
    plain_left.start()
    partial(0)
    merged = []
    for i in range(2):
        o, n = chunks_r[i]
        far_right[i].wait_recv()
        sum_r[pl.ds(o, n)] = relay_r[pl.ds(o, n)] + part[1, pl.ds(o, n)]
        c = remote(sum_r.at[pl.ds(o, n)], far_r.at[pl.ds(o, n)], 6 + i, right)
        c.start()
        merged.append(c)
        o, n = chunks_l[i]
        far_left[i].wait_recv()
        sum_l[pl.ds(o, n)] = relay_l[pl.ds(o, n)] + part[ZHI - 1, pl.ds(split + o, n)]
        c = remote(sum_l.at[pl.ds(o, n)], far_l.at[pl.ds(o, n)], 8 + i, left)
        c.start()
        merged.append(c)
    plain_right.wait()
    plain_left.wait()
    for c in far_right + far_left:
        c.wait_send()
    for c in merged:
        c.wait()
    lo = pl.ds(0, split)
    hi = pl.ds(split, total - split)
    out_ref[lo] = (part[0, lo] + near_l[...] + far_r[...]).astype(out_ref.dtype)
    out_ref[hi] = (part[0, hi] + near_r[...] + far_l[...]).astype(out_ref.dtype)


def born(green, mask, q_table, coupling, occupation, ph_shift):
    edev = green.shape[0]
    lanes = green.shape[3]
    rows = 2 * mask.shape[0] * ORB
    xs = lax.axis_size("kz") // ZHI
    total = edev * rows
    split = (total // 2 + 15) // 16 * 16
    vmem = pltpu.VMEM
    smem = pl.BlockSpec(memory_space=pltpu.SMEM)
    f32 = jnp.float32
    return pl.pallas_call(
        born_kernel,
        out_shape=jax.ShapeDtypeStruct((total, lanes), jnp.bfloat16),
        in_specs=[pl.BlockSpec(memory_space=pl.ANY), pl.BlockSpec(memory_space=vmem), smem, smem, smem, smem],
        out_specs=pl.BlockSpec(memory_space=vmem),
        scratch_shapes=[
            vmem(green.shape, green.dtype),
            pltpu.SemaphoreType.DMA(()),
            vmem((edev, rows, lanes), green.dtype),
            vmem((xs, 3 * edev, rows, lanes), green.dtype),
            vmem((xs, 3 * edev, rows, lanes), f32),
            vmem((ZHI, total, lanes), f32),
            vmem((split, lanes), f32),
            vmem((total - split, lanes), f32),
            vmem((total - split, lanes), f32),
            vmem((split, lanes), f32),
            vmem((split, lanes), f32),
            vmem((total - split, lanes), f32),
            vmem((split, lanes), f32),
            vmem((total - split, lanes), f32),
            pltpu.SemaphoreType.DMA((3 * xs - 1,)),
            pltpu.SemaphoreType.DMA((3 * xs - 1,)),
            pltpu.SemaphoreType.DMA((10,)),
            pltpu.SemaphoreType.DMA((10,)),
        ],
        compiler_params=pltpu.CompilerParams(collective_id=0, has_side_effects=True),
    )(green, mask, q_table, coupling, occupation, ph_shift)


def keldysh_kernel(sig_ref, green_ref, mask_ref, out_ref):
    f32 = jnp.float32
    edev = green_ref.shape[0]
    rows = sig_ref.shape[0] // edev
    members = mask_ref.shape[0]
    width = green_ref.shape[2]
    mask_t = [mask_ref[j].astype(f32).T for j in range(members)]
    tall = lax.broadcasted_iota(jnp.int32, (members * width, rows), 0)
    lane = lax.broadcasted_iota(jnp.int32, (members * width, rows), 1)
    sel = [
        jnp.where(lane - n * members * ORB - ORB * (tall // width) == (tall & (ORB - 1)), 1.0, 0.0).astype(sig_ref.dtype)
        for n in range(2)
    ]

    def nt(a, b):
        return lax.dot_general(a, b, (((1,), (1,)), ((), ())), preferred_element_type=f32)

    for e in range(edev):
        sig = sig_ref[pl.ds(e * rows, rows), :]
        dense_t = []
        for n in range(2):
            tiled = jnp.dot(sel[n], sig, preferred_element_type=f32)
            acc = tiled[0:width] * mask_t[0]
            for j in range(1, members):
                acc = acc + tiled[j * width:(j + 1) * width] * mask_t[j]
            dense_t.append(acc.astype(sig.dtype))
        gr = green_ref[e, 0]
        gi = green_ref[e, 1]
        blocks = nt(jnp.concatenate([gr, gi], 0), jnp.concatenate(dense_t, 0))
        pr = (blocks[:width, :width] - blocks[width:, width:]).astype(gr.dtype)
        pi = (blocks[:width, width:] + blocks[width:, :width]).astype(gr.dtype)
        lhs = jnp.concatenate([jnp.concatenate([pr, pi], 1), jnp.concatenate([pi, -pr], 1)], 0)
        both = nt(lhs, jnp.concatenate([gr, gi], 1))
        out_ref[e, 0] = both[:width].astype(out_ref.dtype)
        out_ref[e, 1] = both[width:].astype(out_ref.dtype)


def keldysh(sigma, green, mask):
    vmem = pl.BlockSpec(memory_space=pltpu.VMEM)
    return pl.pallas_call(
        keldysh_kernel,
        out_shape=jax.ShapeDtypeStruct(green.shape, jnp.bfloat16),
        in_specs=[vmem, vmem, vmem],
        out_specs=vmem,
    )(sigma, green, mask)


def per_device(g_less, g_ret, neighbors, ph_shift, q_table, coupling, occupation):
    width = g_less.shape[4]
    mask = masks(neighbors, width)
    sigma = born(g_less[0, :, 0], mask, q_table, coupling, occupation, ph_shift)
    result = keldysh(sigma, g_ret[0, :, 0, 0], mask)
    return result[None, :, None]


def solution(mesh):
    placed = (
        P("kz", "energy", None, None, None, None),
        P("kz", "energy", None, None, None, None, None),
        P(),
        P(),
        P(),
        P(),
        P(),
    )
    return jax.shard_map(
        per_device,
        mesh=mesh,
        in_specs=placed,
        out_specs=P("kz", "energy", None, None, None, None),
        check_vma=False,
    )
```

```python
import jax
import jax.numpy as jnp
from jax import lax
from jax.experimental import pallas as pl
from jax.experimental.pallas import tpu as pltpu
from jax.sharding import PartitionSpec as P

ORB = 4
NMODE = 2
ZHI = 4


def born_kernel(g_ref, nb_ref, q_ref, c_ref, occ_ref, sh_ref, out_ref, mask_ref, own_ref, land, landf, part, relay_r,
                relay_l, near_r, near_l, far_r, far_l, sum_r, sum_l, gsend, grecv, send, recv):
    kz = lax.axis_index("kz")
    eb = lax.axis_index("energy")
    ne = lax.axis_size("energy")
    momenta = lax.axis_size("kz")
    xs = momenta // ZHI
    x = kz // ZHI
    h = kz % ZHI
    edev = own_ref.shape[0]
    rows = own_ref.shape[1]
    mesh = pl.DeviceIdType.MESH
    peers = [(d, t) for d in range(xs) for t in (-1, 0, 1) if (d, t) != (0, 0)]
    right = x * ZHI + (h + 1) % ZHI
    left = x * ZHI + (h + ZHI - 1) % ZHI

    def where(d, t):
        return {"kz": ((x + d) % xs) * ZHI + h, "energy": (eb + t + ne) % ne}

    barrier = pltpu.get_barrier_semaphore()
    for d, t in peers:
        pl.semaphore_signal(barrier, 1, device_id=where(d, t), device_id_type=mesh)
    for nb in (left, right):
        pl.semaphore_signal(barrier, 1, device_id={"kz": nb}, device_id_type=mesh)

    width = g_ref.shape[2]
    row_atom = lax.broadcasted_iota(jnp.int32, (width, width), 0) // ORB
    col_atom = lax.broadcasted_iota(jnp.int32, (width, width), 1) // ORB
    mask_ref[0] = jnp.where(row_atom == col_atom, 1.0, 0.0).astype(mask_ref.dtype)
    for j in range(1, mask_ref.shape[0]):
        member = jnp.zeros((width, width), jnp.int32)
        for a in range(width // ORB):
            member = jnp.where(row_atom == a, nb_ref[a, j - 1], member)
        mask_ref[j] = jnp.where(member == col_atom, 1.0, 0.0).astype(mask_ref.dtype)

    members = mask_ref.shape[0]
    line = lax.broadcasted_iota(jnp.int32, (rows, width), 0)
    spread = lax.broadcasted_iota(jnp.int32, (rows, width), 1) & (ORB - 1)
    for e in range(edev):
        acc = jnp.zeros((rows, width), jnp.float32)
        for n in range(2):
            green = g_ref[e, n]
            for j in range(members):
                sel_t = jnp.where(line - (n * members + j) * ORB == spread, 1.0, 0.0).astype(green.dtype)
                held = green * mask_ref[j]
                acc = acc + lax.dot_general(
                    sel_t, held, (((1,), (1,)), ((), ())), preferred_element_type=jnp.float32
                )
        own_ref[e] = acc.astype(own_ref.dtype)
        landf[0, edev + e] = acc
    pl.semaphore_wait(barrier, len(peers) + 2)

    copies = []
    for i, (d, t) in enumerate(peers):
        c = pltpu.make_async_remote_copy(
            src_ref=own_ref, dst_ref=land.at[d, pl.ds((1 - t) * edev, edev)],
            send_sem=gsend.at[i], recv_sem=grecv.at[i], device_id=where(d, t), device_id_type=mesh,
        )
        c.start()
        copies.append(c)
    for c in copies:
        c.wait()
    keep = (jnp.where(eb > 0, 1.0, 0.0), 1.0, jnp.where(eb < ne - 1, 1.0, 0.0))
    for d in range(xs):
        for side in range(3):
            if (d, side) == (0, 1):
                continue
            for e in range(edev):
                landf[d, side * edev + e] = land[d, side * edev + e].astype(jnp.float32) * keep[side]

    shifts = [sh_ref[m] for m in range(NMODE)]

    def partial(z):
        k = x * ZHI + (h + z) % ZHI
        weights = []
        for d in range(xs):
            q = q_ref[k, ((x - d + xs) % xs) * ZHI + h]
            for m in range(NMODE):
                w = c_ref[m, q] / momenta
                weights.append((d, m, w * occ_ref[m], w * (occ_ref[m] + 1.0)))
        for e in range(edev):
            acc = jnp.zeros(own_ref.shape[1:], jnp.float32)
            for d, m, wl, wu in weights:
                acc = acc + wl * landf[d, edev + e - shifts[m]]
                acc = acc + wu * landf[d, edev + e + shifts[m]]
            part[z, pl.ds(e * rows, rows)] = acc

    def remote(src, dst, slot, to):
        return pltpu.make_async_remote_copy(
            src_ref=src, dst_ref=dst, send_sem=send.at[slot], recv_sem=recv.at[slot],
            device_id={"kz": to}, device_id_type=mesh,
        )

    total = part.shape[1]
    split = relay_r.shape[0]
    step = split // 2
    chunks_r = [(0, step), (step, split - step)]
    chunks_l = [(0, step), (step, total - split - step)]
    partial(2)
    far_right = [remote(part.at[2, pl.ds(o, n)], relay_r.at[pl.ds(o, n)], i, right)
                 for i, (o, n) in enumerate(chunks_r)]
    far_left = [remote(part.at[2, pl.ds(split + o, n)], relay_l.at[pl.ds(o, n)], 2 + i, left)
                for i, (o, n) in enumerate(chunks_l)]
    for c in far_right + far_left:
        c.start()
    partial(1)
    plain_right = remote(part.at[1, pl.ds(split, total - split)], near_r, 4, right)
    plain_right.start()
    partial(ZHI - 1)
    plain_left = remote(part.at[ZHI - 1, pl.ds(0, split)], near_l, 5, left)
    plain_left.start()
    partial(0)
    merged = []
    for i in range(2):
        o, n = chunks_r[i]
        far_right[i].wait_recv()
        sum_r[pl.ds(o, n)] = relay_r[pl.ds(o, n)] + part[1, pl.ds(o, n)]
        c = remote(sum_r.at[pl.ds(o, n)], far_r.at[pl.ds(o, n)], 6 + i, right)
        c.start()
        merged.append(c)
        o, n = chunks_l[i]
        far_left[i].wait_recv()
        sum_l[pl.ds(o, n)] = relay_l[pl.ds(o, n)] + part[ZHI - 1, pl.ds(split + o, n)]
        c = remote(sum_l.at[pl.ds(o, n)], far_l.at[pl.ds(o, n)], 8 + i, left)
        c.start()
        merged.append(c)
    plain_right.wait()
    plain_left.wait()
    for c in far_right + far_left:
        c.wait_send()
    for c in merged:
        c.wait()
    lo = pl.ds(0, split)
    hi = pl.ds(split, total - split)
    out_ref[lo] = (part[0, lo] + near_l[...] + far_r[...]).astype(out_ref.dtype)
    out_ref[hi] = (part[0, hi] + near_r[...] + far_l[...]).astype(out_ref.dtype)


def born(green, neighbors, q_table, coupling, occupation, ph_shift):
    edev = green.shape[0]
    lanes = green.shape[3]
    members = neighbors.shape[1] + 1
    rows = 2 * members * ORB
    xs = lax.axis_size("kz") // ZHI
    total = edev * rows
    split = (total // 2 + 15) // 16 * 16
    vmem = pltpu.VMEM
    smem = pl.BlockSpec(memory_space=pltpu.SMEM)
    f32 = jnp.float32
    return pl.pallas_call(
        born_kernel,
        out_shape=(
            jax.ShapeDtypeStruct((total, lanes), jnp.bfloat16),
            jax.ShapeDtypeStruct((members, lanes, lanes), jnp.bfloat16),
        ),
        in_specs=[pl.BlockSpec(memory_space=vmem), smem, smem, smem, smem, smem],
        out_specs=(pl.BlockSpec(memory_space=vmem), pl.BlockSpec(memory_space=vmem)),
        scratch_shapes=[
            vmem((edev, rows, lanes), green.dtype),
            vmem((xs, 3 * edev, rows, lanes), green.dtype),
            vmem((xs, 3 * edev, rows, lanes), f32),
            vmem((ZHI, total, lanes), f32),
            vmem((split, lanes), f32),
            vmem((total - split, lanes), f32),
            vmem((total - split, lanes), f32),
            vmem((split, lanes), f32),
            vmem((split, lanes), f32),
            vmem((total - split, lanes), f32),
            vmem((split, lanes), f32),
            vmem((total - split, lanes), f32),
            pltpu.SemaphoreType.DMA((3 * xs - 1,)),
            pltpu.SemaphoreType.DMA((3 * xs - 1,)),
            pltpu.SemaphoreType.DMA((10,)),
            pltpu.SemaphoreType.DMA((10,)),
        ],
        compiler_params=pltpu.CompilerParams(collective_id=0, has_side_effects=True),
    )(green, neighbors, q_table, coupling, occupation, ph_shift)


def keldysh_kernel(sig_ref, green_ref, mask_ref, out_ref):
    f32 = jnp.float32
    edev = green_ref.shape[0]
    rows = sig_ref.shape[0] // edev
    members = mask_ref.shape[0]
    width = green_ref.shape[2]
    mask_t = [mask_ref[j].astype(f32).T for j in range(members)]
    tall = lax.broadcasted_iota(jnp.int32, (members * width, rows), 0)
    lane = lax.broadcasted_iota(jnp.int32, (members * width, rows), 1)
    sel = [
        jnp.where(lane - n * members * ORB - ORB * (tall // width) == (tall & (ORB - 1)), 1.0, 0.0).astype(sig_ref.dtype)
        for n in range(2)
    ]

    def nt(a, b):
        return lax.dot_general(a, b, (((1,), (1,)), ((), ())), preferred_element_type=f32)

    for e in range(edev):
        sig = sig_ref[pl.ds(e * rows, rows), :]
        dense_t = []
        for n in range(2):
            tiled = jnp.dot(sel[n], sig, preferred_element_type=f32)
            acc = tiled[0:width] * mask_t[0]
            for j in range(1, members):
                acc = acc + tiled[j * width:(j + 1) * width] * mask_t[j]
            dense_t.append(acc.astype(sig.dtype))
        gr = green_ref[e, 0]
        gi = green_ref[e, 1]
        blocks = nt(jnp.concatenate([gr, gi], 0), jnp.concatenate(dense_t, 0))
        pr = (blocks[:width, :width] - blocks[width:, width:]).astype(gr.dtype)
        pi = (blocks[:width, width:] + blocks[width:, :width]).astype(gr.dtype)
        lhs = jnp.concatenate([jnp.concatenate([pr, pi], 1), jnp.concatenate([pi, -pr], 1)], 0)
        both = nt(lhs, jnp.concatenate([gr, gi], 1))
        out_ref[e, 0] = both[:width].astype(out_ref.dtype)
        out_ref[e, 1] = both[width:].astype(out_ref.dtype)


def keldysh(sigma, green, mask):
    vmem = pl.BlockSpec(memory_space=pltpu.VMEM)
    return pl.pallas_call(
        keldysh_kernel,
        out_shape=jax.ShapeDtypeStruct(green.shape, jnp.bfloat16),
        in_specs=[vmem, vmem, vmem],
        out_specs=vmem,
    )(sigma, green, mask)


def per_device(g_less, g_ret, neighbors, ph_shift, q_table, coupling, occupation):
    sigma, mask = born(g_less[0, :, 0], neighbors[0], q_table, coupling, occupation, ph_shift)
    result = keldysh(sigma, g_ret[0, :, 0, 0], mask)
    return result[None, :, None]


def solution(mesh):
    placed = (
        P("kz", "energy", None, None, None, None),
        P("kz", "energy", None, None, None, None, None),
        P(),
        P(),
        P(),
        P(),
        P(),
    )
    return jax.shard_map(
        per_device,
        mesh=mesh,
        in_specs=placed,
        out_specs=P("kz", "energy", None, None, None, None),
        check_vma=False,
    )
```

```python
import jax
import jax.numpy as jnp
from jax import lax
from jax.experimental import pallas as pl
from jax.experimental.pallas import tpu as pltpu
from jax.sharding import PartitionSpec as P

ORB = 4
NMODE = 2
ZHI = 4


def born_kernel(g_ref, nb_ref, q_ref, c_ref, occ_ref, sh_ref, out_ref, mask_ref, own_ref, land, landf, part, relay_r,
                relay_l, near_r, near_l, far_r, far_l, sum_r, sum_l, gsend, grecv, send, recv):
    kz = lax.axis_index("kz")
    eb = lax.axis_index("energy")
    ne = lax.axis_size("energy")
    momenta = lax.axis_size("kz")
    xs = momenta // ZHI
    x = kz // ZHI
    h = kz % ZHI
    edev = own_ref.shape[0]
    rows = own_ref.shape[1]
    mesh = pl.DeviceIdType.MESH
    peers = [(d, t) for d in range(xs) for t in (-1, 0, 1) if (d, t) != (0, 0)]
    right = x * ZHI + (h + 1) % ZHI
    left = x * ZHI + (h + ZHI - 1) % ZHI

    def where(d, t):
        return {"kz": ((x + d) % xs) * ZHI + h, "energy": (eb + t + ne) % ne}

    barrier = pltpu.get_barrier_semaphore()
    for d, t in peers:
        pl.semaphore_signal(barrier, 1, device_id=where(d, t), device_id_type=mesh)
    for nb in (left, right):
        pl.semaphore_signal(barrier, 1, device_id={"kz": nb}, device_id_type=mesh)

    width = g_ref.shape[2]
    row_atom = lax.broadcasted_iota(jnp.int32, (width, width), 0) // ORB
    col_atom = lax.broadcasted_iota(jnp.int32, (width, width), 1) // ORB
    mask_ref[0] = jnp.where(row_atom == col_atom, 1.0, 0.0).astype(mask_ref.dtype)
    for j in range(1, mask_ref.shape[0]):
        member = jnp.zeros((width, width), jnp.int32)
        for a in range(width // ORB):
            member = jnp.where(row_atom == a, nb_ref[a, j - 1], member)
        mask_ref[j] = jnp.where(member == col_atom, 1.0, 0.0).astype(mask_ref.dtype)

    members = mask_ref.shape[0]
    line = lax.broadcasted_iota(jnp.int32, (rows, width), 0)
    spread = lax.broadcasted_iota(jnp.int32, (rows, width), 1) & (ORB - 1)
    for e in range(edev):
        acc = jnp.zeros((rows, width), jnp.float32)
        for n in range(2):
            green = g_ref[e, n]
            for j in range(members):
                sel_t = jnp.where(line - (n * members + j) * ORB == spread, 1.0, 0.0).astype(green.dtype)
                held = green * mask_ref[j]
                acc = acc + lax.dot_general(
                    sel_t, held, (((1,), (1,)), ((), ())), preferred_element_type=jnp.float32
                )
        own_ref[e] = acc.astype(own_ref.dtype)
        landf[0, edev + e] = acc
    pl.semaphore_wait(barrier, len(peers) + 2)

    copies = []
    for i, (d, t) in enumerate(peers):
        c = pltpu.make_async_remote_copy(
            src_ref=own_ref, dst_ref=land.at[d, pl.ds((1 - t) * edev, edev)],
            send_sem=gsend.at[i], recv_sem=grecv.at[i], device_id=where(d, t), device_id_type=mesh,
        )
        c.start()
        copies.append(c)
    keep = (jnp.where(eb > 0, 1.0, 0.0), 1.0, jnp.where(eb < ne - 1, 1.0, 0.0))
    for c, (d, t) in zip(copies, peers):
        c.wait()
        side = 1 - t
        for e in range(edev):
            landf[d, side * edev + e] = land[d, side * edev + e].astype(jnp.float32) * keep[side]

    shifts = [sh_ref[m] for m in range(NMODE)]

    def partial(z):
        k = x * ZHI + (h + z) % ZHI
        weights = []
        for d in range(xs):
            q = q_ref[k, ((x - d + xs) % xs) * ZHI + h]
            for m in range(NMODE):
                w = c_ref[m, q] / momenta
                weights.append((d, m, w * occ_ref[m], w * (occ_ref[m] + 1.0)))
        for e in range(edev):
            acc = jnp.zeros(own_ref.shape[1:], jnp.float32)
            for d, m, wl, wu in weights:
                acc = acc + wl * landf[d, edev + e - shifts[m]]
                acc = acc + wu * landf[d, edev + e + shifts[m]]
            part[z, pl.ds(e * rows, rows)] = acc

    def remote(src, dst, slot, to):
        return pltpu.make_async_remote_copy(
            src_ref=src, dst_ref=dst, send_sem=send.at[slot], recv_sem=recv.at[slot],
            device_id={"kz": to}, device_id_type=mesh,
        )

    total = part.shape[1]
    split = relay_r.shape[0]
    step = split // 2
    chunks_r = [(0, step), (step, split - step)]
    chunks_l = [(0, step), (step, total - split - step)]
    partial(2)
    far_right = [remote(part.at[2, pl.ds(o, n)], relay_r.at[pl.ds(o, n)], i, right)
                 for i, (o, n) in enumerate(chunks_r)]
    far_left = [remote(part.at[2, pl.ds(split + o, n)], relay_l.at[pl.ds(o, n)], 2 + i, left)
                for i, (o, n) in enumerate(chunks_l)]
    for c in far_right + far_left:
        c.start()
    partial(1)
    plain_right = remote(part.at[1, pl.ds(split, total - split)], near_r, 4, right)
    plain_right.start()
    partial(ZHI - 1)
    plain_left = remote(part.at[ZHI - 1, pl.ds(0, split)], near_l, 5, left)
    plain_left.start()
    partial(0)
    merged = []
    for i in range(2):
        o, n = chunks_r[i]
        far_right[i].wait_recv()
        sum_r[pl.ds(o, n)] = relay_r[pl.ds(o, n)] + part[1, pl.ds(o, n)]
        c = remote(sum_r.at[pl.ds(o, n)], far_r.at[pl.ds(o, n)], 6 + i, right)
        c.start()
        merged.append(c)
        o, n = chunks_l[i]
        far_left[i].wait_recv()
        sum_l[pl.ds(o, n)] = relay_l[pl.ds(o, n)] + part[ZHI - 1, pl.ds(split + o, n)]
        c = remote(sum_l.at[pl.ds(o, n)], far_l.at[pl.ds(o, n)], 8 + i, left)
        c.start()
        merged.append(c)
    plain_right.wait()
    plain_left.wait()
    for c in far_right + far_left:
        c.wait_send()
    for c in merged:
        c.wait()
    lo = pl.ds(0, split)
    hi = pl.ds(split, total - split)
    out_ref[lo] = (part[0, lo] + near_l[...] + far_r[...]).astype(out_ref.dtype)
    out_ref[hi] = (part[0, hi] + near_r[...] + far_l[...]).astype(out_ref.dtype)


def born(green, neighbors, q_table, coupling, occupation, ph_shift):
    edev = green.shape[0]
    lanes = green.shape[3]
    members = neighbors.shape[1] + 1
    rows = 2 * members * ORB
    xs = lax.axis_size("kz") // ZHI
    total = edev * rows
    split = (total // 2 + 15) // 16 * 16
    vmem = pltpu.VMEM
    smem = pl.BlockSpec(memory_space=pltpu.SMEM)
    f32 = jnp.float32
    return pl.pallas_call(
        born_kernel,
        out_shape=(
            jax.ShapeDtypeStruct((total, lanes), jnp.bfloat16),
            jax.ShapeDtypeStruct((members, lanes, lanes), jnp.bfloat16),
        ),
        in_specs=[pl.BlockSpec(memory_space=vmem), smem, smem, smem, smem, smem],
        out_specs=(pl.BlockSpec(memory_space=vmem), pl.BlockSpec(memory_space=vmem)),
        scratch_shapes=[
            vmem((edev, rows, lanes), green.dtype),
            vmem((xs, 3 * edev, rows, lanes), green.dtype),
            vmem((xs, 3 * edev, rows, lanes), f32),
            vmem((ZHI, total, lanes), f32),
            vmem((split, lanes), f32),
            vmem((total - split, lanes), f32),
            vmem((total - split, lanes), f32),
            vmem((split, lanes), f32),
            vmem((split, lanes), f32),
            vmem((total - split, lanes), f32),
            vmem((split, lanes), f32),
            vmem((total - split, lanes), f32),
            pltpu.SemaphoreType.DMA((3 * xs - 1,)),
            pltpu.SemaphoreType.DMA((3 * xs - 1,)),
            pltpu.SemaphoreType.DMA((10,)),
            pltpu.SemaphoreType.DMA((10,)),
        ],
        compiler_params=pltpu.CompilerParams(collective_id=0, has_side_effects=True),
    )(green, neighbors, q_table, coupling, occupation, ph_shift)


def keldysh_kernel(sig_ref, green_ref, mask_ref, out_ref):
    f32 = jnp.float32
    edev = green_ref.shape[0]
    rows = sig_ref.shape[0] // edev
    members = mask_ref.shape[0]
    width = green_ref.shape[2]
    mask_t = [mask_ref[j].astype(f32).T for j in range(members)]
    tall = lax.broadcasted_iota(jnp.int32, (members * width, rows), 0)
    lane = lax.broadcasted_iota(jnp.int32, (members * width, rows), 1)
    sel = [
        jnp.where(lane - n * members * ORB - ORB * (tall // width) == (tall & (ORB - 1)), 1.0, 0.0).astype(sig_ref.dtype)
        for n in range(2)
    ]

    def nt(a, b):
        return lax.dot_general(a, b, (((1,), (1,)), ((), ())), preferred_element_type=f32)

    for e in range(edev):
        sig = sig_ref[pl.ds(e * rows, rows), :]
        dense_t = []
        for n in range(2):
            tiled = jnp.dot(sel[n], sig, preferred_element_type=f32)
            acc = tiled[0:width] * mask_t[0]
            for j in range(1, members):
                acc = acc + tiled[j * width:(j + 1) * width] * mask_t[j]
            dense_t.append(acc.astype(sig.dtype))
        gr = green_ref[e, 0]
        gi = green_ref[e, 1]
        blocks = nt(jnp.concatenate([gr, gi], 0), jnp.concatenate(dense_t, 0))
        pr = (blocks[:width, :width] - blocks[width:, width:]).astype(gr.dtype)
        pi = (blocks[:width, width:] + blocks[width:, :width]).astype(gr.dtype)
        lhs = jnp.concatenate([jnp.concatenate([pr, pi], 1), jnp.concatenate([pi, -pr], 1)], 0)
        both = nt(lhs, jnp.concatenate([gr, gi], 1))
        out_ref[e, 0] = both[:width].astype(out_ref.dtype)
        out_ref[e, 1] = both[width:].astype(out_ref.dtype)


def keldysh(sigma, green, mask):
    vmem = pl.BlockSpec(memory_space=pltpu.VMEM)
    return pl.pallas_call(
        keldysh_kernel,
        out_shape=jax.ShapeDtypeStruct(green.shape, jnp.bfloat16),
        in_specs=[vmem, vmem, vmem],
        out_specs=vmem,
    )(sigma, green, mask)


def per_device(g_less, g_ret, neighbors, ph_shift, q_table, coupling, occupation):
    sigma, mask = born(g_less[0, :, 0], neighbors[0], q_table, coupling, occupation, ph_shift)
    result = keldysh(sigma, g_ret[0, :, 0, 0], mask)
    return result[None, :, None]


def solution(mesh):
    placed = (
        P("kz", "energy", None, None, None, None),
        P("kz", "energy", None, None, None, None, None),
        P(),
        P(),
        P(),
        P(),
        P(),
    )
    return jax.shard_map(
        per_device,
        mesh=mesh,
        in_specs=placed,
        out_specs=P("kz", "energy", None, None, None, None),
        check_vma=False,
    )
```

```python
import jax
import jax.numpy as jnp
from jax import lax
from jax.experimental import pallas as pl
from jax.experimental.pallas import tpu as pltpu
from jax.sharding import PartitionSpec as P

ORB = 4
NMODE = 2
ZHI = 4


def born_kernel(g_ref, nb_ref, q_ref, c_ref, occ_ref, sh_ref, ret_ref, result_ref, out_ref, mask_ref, own_ref, land, landf, part, relay_r,
                relay_l, near_r, near_l, far_r, far_l, sum_r, sum_l, gsend, grecv, send, recv):
    kz = lax.axis_index("kz")
    eb = lax.axis_index("energy")
    ne = lax.axis_size("energy")
    momenta = lax.axis_size("kz")
    xs = momenta // ZHI
    x = kz // ZHI
    h = kz % ZHI
    edev = own_ref.shape[0]
    rows = own_ref.shape[1]
    mesh = pl.DeviceIdType.MESH
    peers = [(d, t) for d in range(xs) for t in (-1, 0, 1) if (d, t) != (0, 0)]
    right = x * ZHI + (h + 1) % ZHI
    left = x * ZHI + (h + ZHI - 1) % ZHI

    def where(d, t):
        return {"kz": ((x + d) % xs) * ZHI + h, "energy": (eb + t + ne) % ne}

    barrier = pltpu.get_barrier_semaphore()
    for d, t in peers:
        pl.semaphore_signal(barrier, 1, device_id=where(d, t), device_id_type=mesh)
    for nb in (left, right):
        pl.semaphore_signal(barrier, 1, device_id={"kz": nb}, device_id_type=mesh)

    width = g_ref.shape[2]
    row_atom = lax.broadcasted_iota(jnp.int32, (width, width), 0) // ORB
    col_atom = lax.broadcasted_iota(jnp.int32, (width, width), 1) // ORB
    mask_ref[0] = jnp.where(row_atom == col_atom, 1.0, 0.0).astype(mask_ref.dtype)
    for j in range(1, mask_ref.shape[0]):
        member = jnp.zeros((width, width), jnp.int32)
        for a in range(width // ORB):
            member = jnp.where(row_atom == a, nb_ref[a, j - 1], member)
        mask_ref[j] = jnp.where(member == col_atom, 1.0, 0.0).astype(mask_ref.dtype)

    members = mask_ref.shape[0]
    line = lax.broadcasted_iota(jnp.int32, (rows, width), 0)
    spread = lax.broadcasted_iota(jnp.int32, (rows, width), 1) & (ORB - 1)
    for e in range(edev):
        acc = jnp.zeros((rows, width), jnp.float32)
        for n in range(2):
            green = g_ref[e, n]
            for j in range(members):
                sel_t = jnp.where(line - (n * members + j) * ORB == spread, 1.0, 0.0).astype(green.dtype)
                held = green * mask_ref[j]
                acc = acc + lax.dot_general(
                    sel_t, held, (((1,), (1,)), ((), ())), preferred_element_type=jnp.float32
                )
        own_ref[e] = acc.astype(own_ref.dtype)
        landf[0, edev + e] = acc
    pl.semaphore_wait(barrier, len(peers) + 2)

    copies = []
    for i, (d, t) in enumerate(peers):
        c = pltpu.make_async_remote_copy(
            src_ref=own_ref, dst_ref=land.at[d, pl.ds((1 - t) * edev, edev)],
            send_sem=gsend.at[i], recv_sem=grecv.at[i], device_id=where(d, t), device_id_type=mesh,
        )
        c.start()
        copies.append(c)
    for c in copies:
        c.wait()
    keep = (jnp.where(eb > 0, 1.0, 0.0), 1.0, jnp.where(eb < ne - 1, 1.0, 0.0))
    for d in range(xs):
        for side in range(3):
            if (d, side) == (0, 1):
                continue
            for e in range(edev):
                landf[d, side * edev + e] = land[d, side * edev + e].astype(jnp.float32) * keep[side]

    shifts = [sh_ref[m] for m in range(NMODE)]

    def partial(z):
        k = x * ZHI + (h + z) % ZHI
        weights = []
        for d in range(xs):
            q = q_ref[k, ((x - d + xs) % xs) * ZHI + h]
            for m in range(NMODE):
                w = c_ref[m, q] / momenta
                weights.append((d, m, w * occ_ref[m], w * (occ_ref[m] + 1.0)))
        for e in range(edev):
            acc = jnp.zeros(own_ref.shape[1:], jnp.float32)
            for d, m, wl, wu in weights:
                acc = acc + wl * landf[d, edev + e - shifts[m]]
                acc = acc + wu * landf[d, edev + e + shifts[m]]
            part[z, pl.ds(e * rows, rows)] = acc

    def remote(src, dst, slot, to):
        return pltpu.make_async_remote_copy(
            src_ref=src, dst_ref=dst, send_sem=send.at[slot], recv_sem=recv.at[slot],
            device_id={"kz": to}, device_id_type=mesh,
        )

    total = part.shape[1]
    split = relay_r.shape[0]
    step = split // 2
    chunks_r = [(0, step), (step, split - step)]
    chunks_l = [(0, step), (step, total - split - step)]
    partial(2)
    far_right = [remote(part.at[2, pl.ds(o, n)], relay_r.at[pl.ds(o, n)], i, right)
                 for i, (o, n) in enumerate(chunks_r)]
    far_left = [remote(part.at[2, pl.ds(split + o, n)], relay_l.at[pl.ds(o, n)], 2 + i, left)
                for i, (o, n) in enumerate(chunks_l)]
    for c in far_right + far_left:
        c.start()
    partial(1)
    plain_right = remote(part.at[1, pl.ds(split, total - split)], near_r, 4, right)
    plain_right.start()
    partial(ZHI - 1)
    plain_left = remote(part.at[ZHI - 1, pl.ds(0, split)], near_l, 5, left)
    plain_left.start()
    partial(0)
    merged = []
    for i in range(2):
        o, n = chunks_r[i]
        far_right[i].wait_recv()
        sum_r[pl.ds(o, n)] = relay_r[pl.ds(o, n)] + part[1, pl.ds(o, n)]
        c = remote(sum_r.at[pl.ds(o, n)], far_r.at[pl.ds(o, n)], 6 + i, right)
        c.start()
        merged.append(c)
        o, n = chunks_l[i]
        far_left[i].wait_recv()
        sum_l[pl.ds(o, n)] = relay_l[pl.ds(o, n)] + part[ZHI - 1, pl.ds(split + o, n)]
        c = remote(sum_l.at[pl.ds(o, n)], far_l.at[pl.ds(o, n)], 8 + i, left)
        c.start()
        merged.append(c)
    plain_right.wait()
    plain_left.wait()
    for c in far_right + far_left:
        c.wait_send()
    for c in merged:
        c.wait()
    lo = pl.ds(0, split)
    hi = pl.ds(split, total - split)
    out_ref[lo] = (part[0, lo] + near_l[...] + far_r[...]).astype(out_ref.dtype)
    out_ref[hi] = (part[0, hi] + near_r[...] + far_l[...]).astype(out_ref.dtype)
    keldysh_kernel(out_ref, ret_ref, mask_ref, result_ref)


def born(green, neighbors, q_table, coupling, occupation, ph_shift, retarded):
    edev = green.shape[0]
    lanes = green.shape[3]
    members = neighbors.shape[1] + 1
    rows = 2 * members * ORB
    xs = lax.axis_size("kz") // ZHI
    total = edev * rows
    split = (total // 2 + 15) // 16 * 16
    vmem = pltpu.VMEM
    smem = pl.BlockSpec(memory_space=pltpu.SMEM)
    f32 = jnp.float32
    return pl.pallas_call(
        born_kernel,
        out_shape=jax.ShapeDtypeStruct(retarded.shape, jnp.bfloat16),
        in_specs=[pl.BlockSpec(memory_space=vmem), smem, smem, smem, smem, smem, pl.BlockSpec(memory_space=vmem)],
        out_specs=pl.BlockSpec(memory_space=vmem),
        scratch_shapes=[
            vmem((total, lanes), jnp.bfloat16),
            vmem((members, lanes, lanes), jnp.bfloat16),
            vmem((edev, rows, lanes), green.dtype),
            vmem((xs, 3 * edev, rows, lanes), green.dtype),
            vmem((xs, 3 * edev, rows, lanes), f32),
            vmem((ZHI, total, lanes), f32),
            vmem((split, lanes), f32),
            vmem((total - split, lanes), f32),
            vmem((total - split, lanes), f32),
            vmem((split, lanes), f32),
            vmem((split, lanes), f32),
            vmem((total - split, lanes), f32),
            vmem((split, lanes), f32),
            vmem((total - split, lanes), f32),
            pltpu.SemaphoreType.DMA((3 * xs - 1,)),
            pltpu.SemaphoreType.DMA((3 * xs - 1,)),
            pltpu.SemaphoreType.DMA((10,)),
            pltpu.SemaphoreType.DMA((10,)),
        ],
        compiler_params=pltpu.CompilerParams(collective_id=0, has_side_effects=True),
    )(green, neighbors, q_table, coupling, occupation, ph_shift, retarded)


def keldysh_kernel(sig_ref, green_ref, mask_ref, out_ref):
    f32 = jnp.float32
    edev = green_ref.shape[0]
    rows = sig_ref.shape[0] // edev
    members = mask_ref.shape[0]
    width = green_ref.shape[2]
    mask_t = [mask_ref[j].astype(f32).T for j in range(members)]
    tall = lax.broadcasted_iota(jnp.int32, (members * width, rows), 0)
    lane = lax.broadcasted_iota(jnp.int32, (members * width, rows), 1)
    sel = [
        jnp.where(lane - n * members * ORB - ORB * (tall // width) == (tall & (ORB - 1)), 1.0, 0.0).astype(sig_ref.dtype)
        for n in range(2)
    ]

    def nt(a, b):
        return lax.dot_general(a, b, (((1,), (1,)), ((), ())), preferred_element_type=f32)

    for e in range(edev):
        sig = sig_ref[pl.ds(e * rows, rows), :]
        dense_t = []
        for n in range(2):
            tiled = jnp.dot(sel[n], sig, preferred_element_type=f32)
            acc = tiled[0:width] * mask_t[0]
            for j in range(1, members):
                acc = acc + tiled[j * width:(j + 1) * width] * mask_t[j]
            dense_t.append(acc.astype(sig.dtype))
        gr = green_ref[e, 0]
        gi = green_ref[e, 1]
        blocks = nt(jnp.concatenate([gr, gi], 0), jnp.concatenate(dense_t, 0))
        pr = (blocks[:width, :width] - blocks[width:, width:]).astype(gr.dtype)
        pi = (blocks[:width, width:] + blocks[width:, :width]).astype(gr.dtype)
        lhs = jnp.concatenate([jnp.concatenate([pr, pi], 1), jnp.concatenate([pi, -pr], 1)], 0)
        both = nt(lhs, jnp.concatenate([gr, gi], 1))
        out_ref[e, 0] = both[:width].astype(out_ref.dtype)
        out_ref[e, 1] = both[width:].astype(out_ref.dtype)


def keldysh(sigma, green, mask):
    vmem = pl.BlockSpec(memory_space=pltpu.VMEM)
    return pl.pallas_call(
        keldysh_kernel,
        out_shape=jax.ShapeDtypeStruct(green.shape, jnp.bfloat16),
        in_specs=[vmem, vmem, vmem],
        out_specs=vmem,
    )(sigma, green, mask)


def per_device(g_less, g_ret, neighbors, ph_shift, q_table, coupling, occupation):
    result = born(g_less[0, :, 0], neighbors[0], q_table, coupling, occupation, ph_shift, g_ret[0, :, 0, 0])
    return result[None, :, None]


def solution(mesh):
    placed = (
        P("kz", "energy", None, None, None, None),
        P("kz", "energy", None, None, None, None, None),
        P(),
        P(),
        P(),
        P(),
        P(),
    )
    return jax.shard_map(
        per_device,
        mesh=mesh,
        in_specs=placed,
        out_specs=P("kz", "energy", None, None, None, None),
        check_vma=False,
    )
```
